512 devices in a mesh: cfg: 2 (over z_lo), rs: 32 (over x, z_hi, core), tp: 8 (over y).
Axes of the slice: x: 4, y: 8, z: 8 (z_hi: 4, z_lo: 2; z = z_hi * 2 + z_lo), core: 2. Of those that a mesh axis runs over, the one named last changes fastest.
Arguments:
- latents: float32 [8192, 2, 16], P('rs'), may hold values from -6 to 6
- timesteps: int32 [8, 2], replicated, may hold values from 0 to 249
- labels: int32 [8, 2], replicated, may hold values from 0 to 999
- solver_table: float32 [250, 2], replicated, may hold values from 0.5 to 1.5
- time_table: bfloat16 [250, 1152], P(None, 'tp'), may hold values from -6 to 6
- label_table: bfloat16 [1001, 1152], P(None, 'tp'), may hold values from -6 to 6
- patch_weight: bfloat16 [16, 1152], replicated, may hold values from -1.5 to 1.5
- patch_bias: float32 [1152], replicated, may hold values from -3 to 3
- modulation_weight: bfloat16 [9216, 1152], P(('rs', 'tp')), may hold values from -0.1875 to 0.1875
- modulation_bias: float32 [9216], P(('rs', 'tp')), may hold values from -3 to 3
- heads_weight: bfloat16 [1, 1152, 3, 1152], P(None, None, None, 'tp'), may hold values from -0.375 to 0.375
- heads_bias: float32 [1, 3, 1152], P(None, None, 'tp'), may hold values from -1.75 to 1.75
- output_weight: bfloat16 [1, 1152, 1152], P(None, 'tp'), may hold values from -0.1875 to 0.1875
- output_bias: float32 [1, 1152], replicated, may hold values from -1.75 to 1.75
- up_weight: bfloat16 [1, 1152, 4608], P(None, None, 'tp'), may hold values from -0.1875 to 0.1875
- up_bias: float32 [1, 4608], P(None, 'tp'), may hold values from -1.75 to 1.75
- down_weight: bfloat16 [1, 4608, 1152], P(None, 'tp'), may hold values from -0.09375 to 0.09375
- down_bias: float32 [1, 1152], replicated, may hold values from -1.75 to 1.75
- final_weight: bfloat16 [1152, 16], replicated, may hold values from -0.1875 to 0.1875
- final_bias: float32 [16], replicated, may hold values from -1.75 to 1.75
Outputs:
- next_latents: float32 [8192, 2, 16], P(('rs', 'tp'), None, 'cfg')
The draws below stay inside these ranges and needn't reach their ends.
All inputs are finite; a program needn't handle non-finite values.
Results may differ from the reference program's by a relative error of at most 0.02.
Values may be sent and summed in bfloat16 or wider, within the bound.
A program may use at most 64 MiB of HBM per device.

```python
import jax
import jax.numpy as jnp
from jax import lax

D = 1152
HEADS = 16
HEAD_DIM = 72
MLP = 4608
CLASSES = 1000
GRID = 32
PATCH = 16
STEPS = 250
LAYERS = 1
LAT_DEV = 2
SEQ = 1024
GROUPS = 8
MODS = 8
N_TP = 8


def draw_heads_weight(key, part):
    standard = jax.random.truncated_normal(key, -3.0, 3.0, (LAYERS, D, 3, D), jnp.float32) * D ** (-0.5)
    values = standard
    values = jnp.clip(values, -0.375, 0.375)
    values = values.at[0, 0, 2, 0].set(0.375)
    values = values.at[0, 1, 2, 1].set(-0.375)
    return values.astype(jnp.bfloat16)


def plant(array, key, low, largest):
    dims = array.shape
    index_at = [jax.random.randint(jax.random.fold_in(key, axis), (), 0, dims[axis]) for axis in range(len(dims))]
    array = array.at[tuple(index_at)].set(low)
    longest = dims.index(max(dims))
    index_at[longest] = (index_at[longest] + 1) % dims[longest]
    return array.at[tuple(index_at)].set(largest)


def block_scale(rng, dims, shards, smallest, high):
    def one(dim, shards_of):
        heights = jax.random.uniform(jax.random.fold_in(jax.random.fold_in(rng, 6), dim), (shards_of,), jnp.float32, smallest / len(shards), high / len(shards))
        return jnp.repeat(jnp.exp(heights), dims[dim] // shards_of).reshape((-1,) + (1,) * (len(dims) - dim - 1))

    gain = one(*shards[0])
    for cut in shards[1:]:
        gain = gain * one(*cut)
    return gain


def noise(key, dims, scale, limit, shards=(), held_as=jnp.bfloat16):
    drawn = jax.random.normal(key, dims, jnp.float32) * scale
    if len(shards) > 0:
        drawn = block_scale(key, dims, shards, -0.22, 0.18) * drawn
    return jnp.clip(drawn, min=-limit, max=limit).astype(held_as)


def setup_inputs(seed: int = 0) -> dict:
    key_list = jax.random.split(jax.random.key(seed), 21)
    latents = noise(key_list[0], (GROUPS * SEQ, LAT_DEV, PATCH), 1.0, 6.0, ((0, 32),), jnp.float32)
    timesteps = plant(jax.random.randint(key_list[1], (GROUPS, LAT_DEV), 0, STEPS), jax.random.fold_in(key_list[1], 1), 0, STEPS - 1).astype(jnp.int32)
    labels = plant(jax.random.randint(key_list[2], (GROUPS, LAT_DEV), 0, CLASSES), jax.random.fold_in(key_list[2], 1), 0, CLASSES - 1).astype(jnp.int32)
    solver_table = jnp.clip(jax.random.uniform(key_list[3], (STEPS, 2), jnp.float32, 0.5, 1.5), 0.5, 1.5)
    time_table = noise(key_list[4], (STEPS, D), 1.0, 6.0, ((1, 8),))
    label_table = noise(key_list[5], (CLASSES + 1, D), 1.0, 6.0, ((1, 8),))
    patch_weight = noise(key_list[6], (PATCH, D), PATCH ** -0.5, 1.5)
    patch_bias = noise(key_list[7], (D,), 0.5, 3.0, (), jnp.float32)
    modulation_weight = noise(key_list[8], (MODS * D, D), D ** -0.5, 0.1875, ((0, 256),))
    modulation_bias = noise(key_list[9], (MODS * D,), 0.5, 3.0, ((0, 256),), jnp.float32)
    heads_weight = draw_heads_weight(jax.random.fold_in(key_list[20], 71), 0)
    heads_bias = noise(key_list[11], (LAYERS, 3, D), 0.3, 1.75, ((2, 8),), jnp.float32)
    output_weight = noise(key_list[12], (LAYERS, D, D), D ** -0.5, 0.1875, ((1, 8),))
    output_bias = noise(key_list[13], (LAYERS, D), 0.3, 1.75, (), jnp.float32)
    up_weight = noise(key_list[14], (LAYERS, D, MLP), D ** -0.5, 0.1875, ((2, 8),))
    up_bias = noise(key_list[15], (LAYERS, MLP), 0.3, 1.75, ((1, 8),), jnp.float32)
    down_weight = noise(key_list[16], (LAYERS, MLP, D), MLP ** -0.5, 0.09375, ((1, 8),))
    down_bias = noise(key_list[17], (LAYERS, D), 0.3, 1.75, (), jnp.float32)
    final_weight = noise(key_list[18], (D, PATCH), D ** -0.5, 0.1875)
    final_bias = noise(key_list[19], (PATCH,), 0.3, 1.75, (), jnp.float32)
    return {"latents": latents, "timesteps": timesteps, "labels": labels, "solver_table": solver_table, "time_table": time_table, "label_table": label_table, "patch_weight": patch_weight, "patch_bias": patch_bias, "modulation_weight": modulation_weight, "modulation_bias": modulation_bias, "heads_weight": heads_weight, "heads_bias": heads_bias, "output_weight": output_weight, "output_bias": output_bias, "up_weight": up_weight, "up_bias": up_bias, "down_weight": down_weight, "down_bias": down_bias, "final_weight": final_weight, "final_bias": final_bias}


guidance = 4.0

def layer_norm(values):
    centre = values - lax.optimization_barrier(jnp.mean(values, axis=-1, keepdims=True))
    spread = lax.optimization_barrier(jnp.mean(centre * centre, axis=-1, keepdims=True))
    return centre * lax.rsqrt(spread + 1e-06)

def position_rows(token_index, grid_side, model_width):
    freq_count = model_width // 4
    frequency = 1.0 / 10000.0 ** (jnp.arange(freq_count, dtype=jnp.float32) / freq_count)
    row_angle = (token_index // grid_side).astype(jnp.float32)[:, None] * frequency[None, :]
    col_angle = (token_index % grid_side).astype(jnp.float32)[:, None] * frequency[None, :]
    return jnp.concatenate([jnp.sin(row_angle), jnp.cos(row_angle), jnp.sin(col_angle), jnp.cos(col_angle)], axis=1)

def reference(latents, timesteps, labels, solver_table, time_table, label_table, patch_weight, patch_bias, modulation_weight, modulation_bias, heads_weight, heads_bias, output_weight, output_bias, up_weight, up_bias, down_weight, down_bias, final_weight, final_bias):
    grid_tokens = latents.reshape(GROUPS, SEQ, LAT_DEV, PATCH).transpose(0, 2, 1, 3).reshape(GROUPS * LAT_DEV, SEQ, PATCH)
    steps_flat = timesteps.reshape(-1)
    labels_flat = labels.reshape(-1)
    position = position_rows(jnp.arange(SEQ, dtype=jnp.int32), GRID, D)

    def modulation_for(class_ids):
        condition = time_table[steps_flat].astype(jnp.float32) + label_table[class_ids].astype(jnp.float32)
        activation = jax.nn.silu(condition).astype(jnp.bfloat16)
        modulation = jnp.dot(activation, modulation_weight.T, preferred_element_type=jnp.float32) + modulation_bias
        return modulation.reshape(-1, MODS, D)

    def group_sum(rows, weight, groups):
        inner = rows.shape[1] // groups
        split_rows = rows.reshape(SEQ, groups, inner).astype(jnp.float32)
        split_weight = weight.reshape(groups, inner, D).astype(jnp.float32)
        partial_value = jnp.einsum('sgc,gce->gse', split_rows, split_weight)
        partial_value = lax.optimization_barrier(partial_value.astype(jnp.bfloat16)).astype(jnp.float32)
        return lax.optimization_barrier(jnp.sum(partial_value, axis=0))

    def network(latent_item):
        tokens, modulation = latent_item
        stream = jnp.dot(tokens.astype(jnp.bfloat16), patch_weight, preferred_element_type=jnp.float32) + patch_bias + position
        for layer_index in range(LAYERS):
            offset = 6 * layer_index
            normed = (layer_norm(stream) * (1.0 + modulation[offset + 1]) + modulation[offset]).astype(jnp.bfloat16)
            projected = jnp.dot(normed, heads_weight[layer_index].reshape(D, 3 * D), preferred_element_type=jnp.float32) + heads_bias[layer_index].reshape(3 * D)
            projected = lax.optimization_barrier(projected.astype(jnp.bfloat16)).reshape(SEQ, 3, HEADS, HEAD_DIM)
            queries = projected[:, 0].astype(jnp.float32)
            key_rows = projected[:, 1].astype(jnp.float32)
            value_rows = projected[:, 2].astype(jnp.float32)
            scores = jnp.einsum('qhd,khd->hqk', queries, key_rows) * HEAD_DIM ** (-0.5)
            row_top = lax.optimization_barrier(jnp.max(scores, axis=-1, keepdims=True))
            exponent = jnp.exp(scores - row_top)
            row_total = lax.optimization_barrier(jnp.sum(exponent, axis=-1))
            weights = lax.optimization_barrier(exponent.astype(jnp.bfloat16)).astype(jnp.float32)
            attended = jnp.einsum('hqk,khd->qhd', weights, value_rows) / row_total.T[:, :, None]
            attended = attended.astype(jnp.bfloat16).reshape(SEQ, D)
            attn_out = group_sum(attended, output_weight[layer_index], N_TP) + output_bias[layer_index]
            stream = stream + modulation[offset + 2] * attn_out
            normed = (layer_norm(stream) * (1.0 + modulation[offset + 4]) + modulation[offset + 3]).astype(jnp.bfloat16)
            hidden = jnp.dot(normed, up_weight[layer_index], preferred_element_type=jnp.float32) + up_bias[layer_index]
            hidden = jax.nn.gelu(hidden, approximate=True).astype(jnp.bfloat16)
            mlp_out = group_sum(hidden, down_weight[layer_index], N_TP) + down_bias[layer_index]
            stream = stream + modulation[offset + 5] * mlp_out
        final_offset = 6 * LAYERS
        normed = (layer_norm(stream) * (1.0 + modulation[final_offset + 1]) + modulation[final_offset]).astype(jnp.bfloat16)
        return jnp.dot(normed, final_weight, preferred_element_type=jnp.float32) + final_bias
    cond_modulation = modulation_for(labels_flat)
    uncond_modulation = modulation_for(jnp.full_like(labels_flat, CLASSES))
    cond_noise = lax.map(network, (grid_tokens, cond_modulation))
    uncond_noise = lax.map(network, (grid_tokens, uncond_modulation))
    guided = uncond_noise + guidance * (cond_noise - uncond_noise)
    coefficients = solver_table[steps_flat]
    result = coefficients[:, 0, None, None] * grid_tokens + coefficients[:, 1, None, None] * guided
    return result.reshape(GROUPS, LAT_DEV, SEQ, PATCH).transpose(0, 2, 1, 3).reshape(GROUPS * SEQ, LAT_DEV, PATCH)
```

```python
import functools

import jax
import jax.numpy as jnp
import numpy as np
from jax import lax
from jax.experimental import pallas as pl
from jax.experimental.pallas import tpu as pltpu
from jax.sharding import PartitionSpec as P

HEAD_DIM = 72
GRID = 32
D = 1152
LANES = 128
GUIDANCE = 4.0
MESH = pl.DeviceIdType.MESH
F32, BF16 = jnp.float32, jnp.bfloat16


def remote(src, dst, send, recv, device):
    return pltpu.make_async_remote_copy(
        src_ref=src, dst_ref=dst, send_sem=send, recv_sem=recv, device_id=device, device_id_type=MESH
    )


def layer_norm(values):
    centre = values - jnp.mean(values, axis=-1, keepdims=True)
    spread = jnp.mean(centre * centre, axis=-1, keepdims=True)
    return centre * lax.rsqrt(spread + 1e-06)


def position_tables():
    count = D // 4
    frequency = 1.0 / 10000.0 ** (np.arange(count, dtype=np.float64) / count)
    angle = np.arange(GRID, dtype=np.float64)[:, None] * frequency[None, :]
    half = np.concatenate([np.sin(angle), np.cos(angle)], axis=1)
    zero = np.zeros_like(half)
    row = np.concatenate([half, zero], axis=1).astype(np.float32)
    col = np.concatenate([zero, half], axis=1).astype(np.float32)
    return row, col


def conditioning_kernel(
    tp_n, rs_n, cond_ref, w_ref, b_ref, lat_ref, out_ref, latall_ref,
    cbuf, part, pbuf, blk, obuf, lbuf, s1, r1, s2, r2, s3, r3, s4, r4,
):
    tp, rs = lax.axis_index("tp"), lax.axis_index("rs")
    quarter, base = rs % 4, (rs // 4) * 4
    barrier = pltpu.get_barrier_semaphore()
    for d in range(1, tp_n):
        pl.semaphore_signal(barrier, inc=1, device_id={"tp": (tp + d) % tp_n}, device_id_type=MESH)
    for d in range(1, rs_n):
        pl.semaphore_signal(barrier, inc=1, device_id={"rs": (rs + d) % rs_n}, device_id_type=MESH)
    pl.semaphore_wait(barrier, tp_n - 1 + rs_n - 1)

    first = []
    for d in range(1, tp_n):
        c = remote(cond_ref, cbuf.at[tp], s1.at[d], r1.at[d], {"tp": (tp + d) % tp_n})
        c.start()
        first.append(c)
    lats = []
    for d in range(1, 4):
        c = remote(lat_ref, lbuf.at[d], s4.at[d], r4.at[d], {"rs": base + (quarter + d) % 4})
        c.start()
        lats.append(c)
    cbuf[tp] = cond_ref[...]
    for c in first:
        c.wait()
    total = jnp.broadcast_to(b_ref[...], (cond_ref.shape[0], LANES))
    for t in range(tp_n):
        v = cbuf[t]
        act = (v / (1.0 + jnp.exp(-v))).astype(BF16)
        total = total + lax.dot_general(
            act, w_ref[t], (((1,), (1,)), ((), ())), preferred_element_type=F32
        )
    part[...] = total
    second = []
    for d in range(1, tp_n):
        c = remote(part, pbuf.at[tp], s2.at[d], r2.at[d], {"tp": (tp + d) % tp_n})
        c.start()
        second.append(c)
    pbuf[tp] = total
    for c in second:
        c.wait()
    share = D * 8 // (tp_n * rs_n)
    rows = jnp.concatenate([pbuf[t][:, :share] for t in range(tp_n)], axis=1)
    for g in range(blk.shape[0]):
        blk[g, :, : rows.shape[1]] = rows[2 * g : 2 * g + 2, :]
    third = []
    for d in range(1, rs_n):
        peer = (rs + d) % rs_n
        c = remote(blk.at[peer // 4], obuf.at[rs], s3.at[d], r3.at[d], {"rs": peer})
        c.start()
        third.append(c)
    obuf[rs] = blk[rs // 4]
    latall_ref[0] = lat_ref[...]
    for d in range(1, 4):
        lats[d - 1].wait()
        latall_ref[d] = lbuf[d]
    for c in third:
        c.wait()
    out_ref[...] = obuf[...]


def conditioning(cond, weight, bias, lat, tp_n, rs_n):
    n = cond.shape[0]
    wide = 3 * LANES
    vmem = pl.BlockSpec(memory_space=pltpu.VMEM)
    dma = pltpu.SemaphoreType.DMA
    return pl.pallas_call(
        functools.partial(conditioning_kernel, tp_n, rs_n),
        out_shape=(
            jax.ShapeDtypeStruct((rs_n, 2, wide), F32),
            jax.ShapeDtypeStruct((4,) + lat.shape, BF16),
        ),
        in_specs=[vmem] * 4,
        out_specs=(vmem, vmem),
        scratch_shapes=[
            pltpu.VMEM((tp_n,) + cond.shape, F32),
            pltpu.VMEM((n, LANES), F32),
            pltpu.VMEM((tp_n, n, LANES), F32),
            pltpu.VMEM((n // 2, 2, wide), F32),
            pltpu.VMEM((rs_n, 2, wide), F32),
            pltpu.VMEM((4,) + lat.shape, BF16),
            dma((tp_n,)), dma((tp_n,)), dma((tp_n,)), dma((tp_n,)),
            dma((rs_n,)), dma((rs_n,)), dma((4,)), dma((4,)),
        ],
        compiler_params=pltpu.CompilerParams(collective_id=0, has_side_effects=True),
        name="conditioning",
    )(cond, weight, bias, lat)


def attention_kernel(lat_ref, pw_ref, col_ref, row_ref, mod_ref, wq_ref, wkv_ref, bq_ref, bkv_ref,
                     wo_ref, out_ref, normed, kv):
    tile = 256

    def fill(step, latent, slot):
        emb = jnp.dot(
            lat_ref[latent, pl.ds(pl.multiple_of(slot * tile, tile), tile), :],
            pw_ref[...], preferred_element_type=F32,
        )
        shift, scale = mod_ref[latent, 0:1, :], 1.0 + mod_ref[latent, 1:2, :]
        for i in range(tile // GRID):
            stream = (emb[i * GRID : (i + 1) * GRID] + col_ref[...]) + row_ref[slot, i : i + 1, :]
            normed[i * GRID : (i + 1) * GRID, :] = (
                layer_norm(stream) * scale + shift
            ).astype(BF16)
        pair = jnp.dot(normed[...], wkv_ref[...], preferred_element_type=F32) + bkv_ref[...]
        kv[pl.ds(pl.multiple_of(slot * tile, tile), tile), :] = pair.astype(BF16)

    @pl.loop(0, 2)
    def _(latent):
        @pl.loop(0, 4)
        def _(step):
            fill(step, latent, 3 - step)

        queries = (
            jnp.dot(normed[...], wq_ref[...], preferred_element_type=F32) + bq_ref[...]
        ).astype(BF16)
        total = None
        for h in range(2):
            q = queries[:, h * LANES : (h + 1) * LANES]
            k = kv[:, h * LANES : (h + 1) * LANES]
            v = kv[:, (2 + h) * LANES : (3 + h) * LANES]
            scores = lax.dot_general(
                q, k, (((1,), (1,)), ((), ())), preferred_element_type=F32
            ) * HEAD_DIM ** (-0.5)
            exponent = jnp.exp(scores - jnp.max(scores, axis=-1, keepdims=True))
            row_total = jnp.sum(exponent, axis=-1, keepdims=True)
            weighted = jnp.dot(exponent.astype(BF16), v, preferred_element_type=F32)
            attended = (weighted / row_total).astype(BF16)
            term = jnp.dot(attended, wo_ref[h], preferred_element_type=F32)
            total = term if total is None else total + term
        result = total.astype(BF16)
        for t in range(8):
            out_ref[t, latent] = result[t * GRID : (t + 1) * GRID, :]


def attention(lat, pw, col, row, mod, wq, wkv, bq, bkv, wo):
    vmem = pl.BlockSpec(memory_space=pltpu.VMEM)
    return pl.pallas_call(
        attention_kernel,
        out_shape=jax.ShapeDtypeStruct((8, 2, GRID, D), BF16),
        in_specs=[vmem] * 10,
        out_specs=vmem,
        scratch_shapes=[pltpu.VMEM((256, D), BF16), pltpu.VMEM((1024, 4 * LANES), BF16)],
        compiler_params=pltpu.CompilerParams(vmem_limit_bytes=60000000),
        name="attention",
    )(lat, pw, col, row, mod, wq, wkv, bq, bkv, wo)


def feed_kernel(
    n, part_ref, lat_ref, latb_ref, pw_ref, pos_ref, mod_ref, ob_ref, up_ref, upb_ref, down_ref,
    downb_ref, fw_ref, fb_ref, c0_ref, c1_ref, out_ref,
    r1, gathered, held, r2, stream_ref, own, noise, other,
    s1, q1, sr, qr, sl, ql, s2, q2, s3, q3,
):
    me, half = lax.axis_index("tp"), lax.axis_index("cfg")
    barrier = pltpu.get_barrier_semaphore()
    for d in range(1, n):
        pl.semaphore_signal(barrier, inc=1, device_id={"tp": (me + d) % n}, device_id_type=MESH)
    pl.semaphore_signal(barrier, inc=1, device_id={"cfg": 1 - half}, device_id_type=MESH)
    pl.semaphore_wait(barrier, n)

    sent = []
    for d in (4, 3, 5, 2, 6, 1, 7):
        peer = (me + d) % n
        c = remote(part_ref.at[peer], r1.at[d], s1.at[d], q1.at[d], {"tp": peer})
        c.start()
        sent.append((d, c))
    rows = GRID

    def mods(m):
        return [mod_ref[l, m : m + 1, :] for l in range(2)]

    def both(rows_of):
        return jnp.concatenate([rows_of(0), rows_of(1)], axis=0)

    def modulated(stream, o):
        shift, scale = mods(o), mods(o + 1)
        normed = layer_norm(stream)
        return both(
            lambda l: (normed[l * rows : (l + 1) * rows] * (1.0 + scale[l]) + shift[l]).astype(BF16)
        )

    def gated(stream, o, value):
        gate = mods(o)
        return both(
            lambda l: stream[l * rows : (l + 1) * rows] + gate[l] * value[l * rows : (l + 1) * rows]
        )

    stream_ref[...] = (
        jnp.dot(latb_ref[...], pw_ref[...], preferred_element_type=F32)
        + jnp.concatenate([pos_ref[...], pos_ref[...]], axis=0)
    )
    total = part_ref[me].astype(F32)
    for d, c in reversed(sent):
        c.wait()
        total = total + r1[d].astype(F32)
    stream = gated(stream_ref[...], 2, total + ob_ref[...])
    stream_ref[...] = stream
    gathered[me] = modulated(stream, 3)

    right, left = {"tp": (me + 1) % n}, {"tp": (me + n - 1) % n}

    def hop(k):
        held_r, held_l = (me - (k - 1) + n) % n, (me + (k - 1)) % n
        out = [remote(gathered.at[held_r], gathered.at[held_r], sr.at[k], qr.at[k], right)]
        if k < n // 2:
            out.append(remote(gathered.at[held_l], gathered.at[held_l], sl.at[k], ql.at[k], left))
        for c in out:
            c.start()
        return out

    def units(x):
        pre = jnp.dot(x, up_ref[...], preferred_element_type=F32) + upb_ref[...]
        hid = jax.nn.gelu(pre, approximate=True).astype(BF16)
        return jnp.dot(hid, down_ref[...], preferred_element_type=F32).astype(BF16)

    flying = []

    def give(k, value):
        held[k] = value
        peer = (me - k + n) % n
        c = remote(held.at[k], r2.at[k], s2.at[k], q2.at[k], {"tp": peer})
        c.start()
        flying.append((k, c))

    hops = hop(1)
    own[...] = units(gathered[me])
    for k in range(1, n // 2 + 1):
        for c in hops:
            c.wait()
        if k < n // 2:
            hops = hop(k + 1)
            x = jnp.concatenate([gathered[(me - k + n) % n], gathered[(me + k) % n]], axis=0)
            y = units(x)
            give(k, y[: 2 * rows])
            give(n - k, y[2 * rows :])
        else:
            give(k, units(gathered[(me - k + n) % n]))

    total = own[...].astype(F32)
    for k, c in flying:
        c.wait()
        total = total + r2[k].astype(F32)
    stream = gated(stream_ref[...], 5, total + downb_ref[...])
    value = jnp.dot(modulated(stream, 6), fw_ref[...], preferred_element_type=F32) + fb_ref[...]
    noise[...] = value
    c = remote(noise, other, s3, q3, {"cfg": 1 - half})
    c.start()
    c.wait()
    theirs = other[...]
    first = half == 0
    conditional = jnp.where(first, value, theirs)
    unconditional = jnp.where(first, theirs, value)
    guided = unconditional + GUIDANCE * (conditional - unconditional)
    out_ref[...] = c0_ref[...] * lat_ref[...] + c1_ref[...] * guided


def feed(n, *operands):
    vmem = pl.BlockSpec(memory_space=pltpu.VMEM)
    dma = pltpu.SemaphoreType.DMA
    rows = 2 * GRID
    return pl.pallas_call(
        functools.partial(feed_kernel, n),
        out_shape=jax.ShapeDtypeStruct((rows, LANES), F32),
        in_specs=[vmem] * len(operands),
        out_specs=vmem,
        scratch_shapes=[
            pltpu.VMEM((n, rows, D), BF16),
            pltpu.VMEM((n, rows, D), BF16),
            pltpu.VMEM((n, rows, D), BF16),
            pltpu.VMEM((n, rows, D), BF16),
            pltpu.VMEM((rows, D), F32),
            pltpu.VMEM((rows, D), BF16),
            pltpu.VMEM((rows, LANES), F32),
            pltpu.VMEM((rows, LANES), F32),
        ] + [dma((n,))] * 8 + [dma(()), dma(())],
        compiler_params=pltpu.CompilerParams(
            collective_id=1, has_side_effects=True, vmem_limit_bytes=60000000
        ),
        name="feed",
    )(*operands)


def pad_heads(value):
    split = value.reshape(value.shape[:-1] + (2, HEAD_DIM))
    wide = jnp.pad(split, [(0, 0)] * (split.ndim - 1) + [(0, LANES - HEAD_DIM)])
    return wide.reshape(value.shape[:-1] + (2 * LANES,))


def per_device(
    latents, timesteps, labels, solver_table, time_table, label_table, patch_weight, patch_bias,
    modulation_weight, modulation_bias, heads_weight, heads_bias, output_weight, output_bias,
    up_weight, up_bias, down_weight, down_bias, final_weight, final_bias,
):
    tp_n, rs_n = lax.axis_size("tp"), lax.axis_size("rs")
    tp, half, rs = lax.axis_index("tp"), lax.axis_index("cfg"), lax.axis_index("rs")
    group, quarter = rs // 4, rs % 4
    classes = label_table.shape[0] - 1
    local, latents_dev, patch = latents.shape
    share = local // tp_n

    class_ids = jnp.where(half == 0, labels.reshape(-1), classes)
    step_onehot = jax.nn.one_hot(timesteps.reshape(-1), time_table.shape[0], dtype=BF16)
    class_onehot = jax.nn.one_hot(class_ids, classes + 1, dtype=BF16)
    cond = jnp.dot(step_onehot, time_table, preferred_element_type=F32) + jnp.dot(
        class_onehot, label_table, preferred_element_type=F32
    )
    mine = D // tp_n
    cond = jnp.pad(cond, ((0, 0), (0, 2 * LANES - mine)))
    mrows = modulation_weight.shape[0]
    mw = jnp.transpose(modulation_weight.reshape(mrows, tp_n, mine), (1, 0, 2))
    mw = jnp.pad(mw, ((0, 0), (0, LANES - mrows), (0, 2 * LANES - mine)))
    mb = jnp.pad(modulation_bias, (0, LANES - mrows)).reshape(1, LANES)
    lat_t = jnp.transpose(latents.astype(BF16), (1, 2, 0)).reshape(latents_dev * patch, local)
    mod, lat_all = conditioning(cond, mw, mb, lat_t, tp_n, rs_n)
    width = mrows * tp_n
    mod = mod[:, :, :width].reshape(8, rs_n // 8, 2, width)
    mod = jnp.transpose(mod, (2, 0, 1, 3)).reshape(2, 8, D)

    row_np, col_np = position_tables()
    row_table = jnp.asarray(row_np)
    col_bias = jnp.asarray(col_np) + patch_bias[None, :]
    slots = (quarter + 4 - jnp.arange(4)) % 4
    row_slots = jnp.take(row_table.reshape(4, 8, D), slots, axis=0)
    lat_all = jnp.transpose(
        lat_all.reshape(4, latents_dev, patch, local), (1, 0, 3, 2)
    ).reshape(latents_dev, 4 * local, patch)

    hw, hb = heads_weight[0], heads_bias[0]
    wq = pad_heads(hw[:, 0])
    wkv = jnp.concatenate([pad_heads(hw[:, 1]), pad_heads(hw[:, 2])], axis=1)
    bq = pad_heads(hb[0]).reshape(1, -1)
    bkv = jnp.concatenate([pad_heads(hb[1]), pad_heads(hb[2])]).reshape(1, -1)
    wo = jnp.pad(
        output_weight[0].reshape(2, HEAD_DIM, D), ((0, 0), (0, LANES - HEAD_DIM), (0, 0))
    )
    partial = attention(
        lat_all, patch_weight, col_bias, row_slots, mod, wq, wkv, bq, bkv, wo
    ).reshape(8, 2 * GRID, D)

    own = lax.dynamic_slice_in_dim(latents, tp * share, share, 0)
    own = jnp.transpose(own, (1, 0, 2)).reshape(2 * share, patch)
    pos = col_bias + lax.dynamic_slice_in_dim(row_table, quarter * 8 + tp, 1, 0)
    step_own = lax.dynamic_index_in_dim(timesteps, group, 0, keepdims=False)
    hot = jax.nn.one_hot(step_own, solver_table.shape[0], dtype=F32)
    coef = jnp.dot(hot, solver_table, precision=lax.Precision.HIGHEST)
    coef = jnp.repeat(coef, share, axis=0)
    out = feed(
        tp_n, partial, jnp.pad(own, ((0, 0), (0, LANES - patch))), own.astype(BF16), patch_weight,
        pos, mod, output_bias, up_weight[0], up_bias, down_weight[0], down_bias,
        jnp.pad(final_weight, ((0, 0), (0, LANES - patch))),
        jnp.pad(final_bias, (0, LANES - patch)).reshape(1, LANES), coef[:, 0:1], coef[:, 1:2],
    )
    kept = lax.dynamic_slice_in_dim(out[:, :patch], half * (patch // 2), patch // 2, 1)
    return jnp.transpose(kept.reshape(latents_dev, share, patch // 2), (1, 0, 2))


def solution(mesh):
    in_specs = (
        P("rs", None, None), P(), P(), P(), P(None, "tp"), P(None, "tp"), P(), P(),
        P(("rs", "tp"), None), P(("rs", "tp")), P(None, None, None, "tp"), P(None, None, "tp"),
        P(None, "tp", None), P(), P(None, None, "tp"), P(None, "tp"), P(None, "tp", None), P(),
        P(), P(),
    )
    return jax.shard_map(
        per_device, mesh=mesh, in_specs=in_specs,
        out_specs=P(("rs", "tp"), None, "cfg"), check_vma=False,
    )
```

```python
import functools

import jax
import jax.numpy as jnp
import numpy as np
from jax import lax
from jax.experimental import pallas as pl
from jax.experimental.pallas import tpu as pltpu
from jax.sharding import PartitionSpec as P

HEAD_DIM = 72
GRID = 32
D = 1152
LANES = 128
GUIDANCE = 4.0
MESH = pl.DeviceIdType.MESH
F32, BF16 = jnp.float32, jnp.bfloat16


def remote(src, dst, send, recv, device):
    return pltpu.make_async_remote_copy(
        src_ref=src, dst_ref=dst, send_sem=send, recv_sem=recv, device_id=device, device_id_type=MESH
    )


def layer_norm(values):
    centre = values - jnp.mean(values, axis=-1, keepdims=True)
    spread = jnp.mean(centre * centre, axis=-1, keepdims=True)
    return centre * lax.rsqrt(spread + 1e-06)


def position_tables():
    count = D // 4
    frequency = 1.0 / 10000.0 ** (np.arange(count, dtype=np.float64) / count)
    angle = np.arange(GRID, dtype=np.float64)[:, None] * frequency[None, :]
    half = np.concatenate([np.sin(angle), np.cos(angle)], axis=1)
    zero = np.zeros_like(half)
    row = np.concatenate([half, zero], axis=1).astype(np.float32)
    col = np.concatenate([zero, half], axis=1).astype(np.float32)
    return row, col


def conditioning_kernel(
    tp_n, rs_n, cond_ref, w_ref, b_ref, lat_ref, out_ref, latall_ref,
    cbuf, part, pbuf, blk, gbuf, obuf, lbuf, s1, r1, s2, r2, s3, r3, s4, r4, s5, r5,
):
    tp, rs = lax.axis_index("tp"), lax.axis_index("rs")
    quarter, group, groups = rs % 4, rs // 4, rs_n // 4
    barrier = pltpu.get_barrier_semaphore()

    def at_tp(d):
        return {"tp": (tp + d) % tp_n}

    def at_quarter(d):
        return {"rs": group * 4 + (quarter + d) % 4}

    def at_group(d):
        return {"rs": ((group + d) % groups) * 4 + quarter}

    for d in range(1, tp_n):
        pl.semaphore_signal(barrier, inc=1, device_id=at_tp(d), device_id_type=MESH)
    for d in range(1, groups):
        pl.semaphore_signal(barrier, inc=1, device_id=at_group(d), device_id_type=MESH)
    for d in range(1, 4):
        pl.semaphore_signal(barrier, inc=1, device_id=at_quarter(d), device_id_type=MESH)
    pl.semaphore_wait(barrier, tp_n - 1 + groups - 1 + 3)

    first = []
    for d in range(1, tp_n):
        c = remote(cond_ref, cbuf.at[tp], s1.at[d], r1.at[d], at_tp(d))
        c.start()
        first.append(c)
    lats = []
    for d in range(1, 4):
        c = remote(lat_ref, lbuf.at[d], s4.at[d], r4.at[d], at_quarter(d))
        c.start()
        lats.append(c)
    cbuf[tp] = cond_ref[...]
    latall_ref[0] = lat_ref[...]
    for c in first:
        c.wait()
    total = jnp.broadcast_to(b_ref[...], (cond_ref.shape[0], LANES))
    for t in range(tp_n):
        v = cbuf[t]
        act = (v / (1.0 + jnp.exp(-v))).astype(BF16)
        total = total + lax.dot_general(
            act, w_ref[t], (((1,), (1,)), ((), ())), preferred_element_type=F32
        )
    part[...] = total
    second = []
    for d in range(1, tp_n):
        c = remote(part, pbuf.at[tp], s2.at[d], r2.at[d], at_tp(d))
        c.start()
        second.append(c)
    pbuf[tp] = total
    for d in range(1, 4):
        lats[d - 1].wait()
        latall_ref[d] = lbuf[d]
    for c in second:
        c.wait()
    share = D * 8 // (tp_n * rs_n)
    rows = jnp.concatenate([pbuf[t][:, :share] for t in range(tp_n)], axis=1)
    width = rows.shape[1]
    rows = jnp.concatenate([rows, jnp.zeros((rows.shape[0], 3 * LANES - width), F32)], axis=1)
    for g in range(groups):
        blk[g] = rows[2 * g : 2 * g + 2, :]
    third = []
    for d in range(1, groups):
        c = remote(blk.at[(group + d) % groups], gbuf.at[group], s3.at[d], r3.at[d], at_group(d))
        c.start()
        third.append(c)
    gbuf[group] = blk[group]
    for c in third:
        c.wait()
    fourth = []
    for d in range(1, 4):
        c = remote(gbuf, obuf.at[quarter], s5.at[d], r5.at[d], at_quarter(d))
        c.start()
        fourth.append(c)
    obuf[quarter] = gbuf[...]
    for c in fourth:
        c.wait()
    for l in range(2):
        out_ref[l] = jnp.concatenate([obuf[q, :, l, :][:, :width] for q in range(4)], axis=1)


def conditioning(cond, weight, bias, lat, tp_n, rs_n):
    n = cond.shape[0]
    wide, groups = 3 * LANES, rs_n // 4
    vmem = pl.BlockSpec(memory_space=pltpu.VMEM)
    dma = pltpu.SemaphoreType.DMA
    return pl.pallas_call(
        functools.partial(conditioning_kernel, tp_n, rs_n),
        out_shape=(
            jax.ShapeDtypeStruct((2, groups, D), F32),
            jax.ShapeDtypeStruct((4,) + lat.shape, BF16),
        ),
        in_specs=[vmem] * 4,
        out_specs=(vmem, vmem),
        scratch_shapes=[
            pltpu.VMEM((tp_n,) + cond.shape, F32),
            pltpu.VMEM((n, LANES), F32),
            pltpu.VMEM((tp_n, n, LANES), F32),
            pltpu.VMEM((groups, 2, wide), F32),
            pltpu.VMEM((groups, 2, wide), F32),
            pltpu.VMEM((4, groups, 2, wide), F32),
            pltpu.VMEM((4,) + lat.shape, BF16),
            dma((tp_n,)), dma((tp_n,)), dma((tp_n,)), dma((tp_n,)),
            dma((groups,)), dma((groups,)), dma((4,)), dma((4,)), dma((4,)), dma((4,)),
        ],
        compiler_params=pltpu.CompilerParams(collective_id=0, has_side_effects=True),
        name="conditioning",
    )(cond, weight, bias, lat)


def attention_kernel(lat_ref, pw_ref, pb_ref, col_ref, row_ref, mod_ref, w_ref, b_ref,
                     wo_ref, out_ref, normed, kv):
    tile, wide = 256, 2 * LANES
    quarter = lax.axis_index("rs") % 4

    def fill(latent, slot):
        emb = lax.dot_general(
            lat_ref[slot, latent], pw_ref[...], (((0,), (0,)), ((), ())),
            preferred_element_type=F32,
        )
        shift, scale = mod_ref[latent, 0:1, :], 1.0 + mod_ref[latent, 1:2, :]
        col = col_ref[...] + pb_ref[...]
        place = pl.multiple_of(((quarter + 4 - slot) % 4) * 8, 8)
        row = row_ref[pl.ds(place, 8), :]
        for i in range(tile // GRID):
            stream = (emb[i * GRID : (i + 1) * GRID] + col) + row[i : i + 1, :]
            normed[i * GRID : (i + 1) * GRID, :] = (
                layer_norm(stream) * scale + shift
            ).astype(BF16)
        pair = jnp.dot(normed[...], w_ref[:, wide:], preferred_element_type=F32) + b_ref[:, wide:]
        kv[pl.ds(pl.multiple_of(slot * tile, tile), tile), :] = pair.astype(BF16)

    @pl.loop(0, 2)
    def _(latent):
        @pl.loop(0, 4)
        def _(step):
            fill(latent, 3 - step)

        queries = (
            jnp.dot(normed[...], w_ref[:, :wide], preferred_element_type=F32) + b_ref[:, :wide]
        )
        lane = lax.broadcasted_iota(jnp.int32, (tile, wide), 1)
        heads = []
        for h in range(2):
            inside = (lane >= h * HEAD_DIM) & (lane < (h + 1) * HEAD_DIM)
            q = jnp.where(inside, queries, 0.0).astype(BF16)
            scores = lax.dot_general(
                q, kv[:, :wide], (((1,), (1,)), ((), ())), preferred_element_type=F32
            ) * HEAD_DIM ** (-0.5)
            exponent = jnp.exp(scores - jnp.max(scores, axis=-1, keepdims=True))
            row_total = jnp.sum(exponent, axis=-1, keepdims=True)
            weighted = jnp.dot(exponent.astype(BF16), kv[:, wide:], preferred_element_type=F32)
            heads.append(weighted / row_total)
        attended = jnp.where(lane < HEAD_DIM, heads[0], heads[1]).astype(BF16)
        result = jnp.dot(
            attended[:, : 2 * HEAD_DIM], wo_ref[...], preferred_element_type=F32
        ).astype(BF16)
        for t in range(8):
            out_ref[t, latent] = result[t * GRID : (t + 1) * GRID, :]


def attention(*operands):
    vmem = pl.BlockSpec(memory_space=pltpu.VMEM)
    return pl.pallas_call(
        attention_kernel,
        out_shape=jax.ShapeDtypeStruct((8, 2, GRID, D), BF16),
        in_specs=[vmem] * len(operands),
        out_specs=vmem,
        scratch_shapes=[pltpu.VMEM((256, D), BF16), pltpu.VMEM((1024, 4 * LANES), BF16)],
        compiler_params=pltpu.CompilerParams(vmem_limit_bytes=60000000),
        name="attention",
    )(*operands)


def feed_kernel(
    n, part_ref, lat_ref, pw_ref, pb_ref, col_ref, row_ref, mod_ref, ob_ref, up_ref, upb_ref,
    down_ref, downb_ref, fw_ref, fb_ref, c0_ref, c1_ref, out_ref,
    chain, gathered, held, r2, stream_ref, own, noise, other,
    s1, q1, sr, qr, sl, ql, s2, q2, s3, q3,
):
    me, half = lax.axis_index("tp"), lax.axis_index("cfg")
    barrier = pltpu.get_barrier_semaphore()
    for d in range(1, n):
        pl.semaphore_signal(barrier, inc=1, device_id={"tp": (me + d) % n}, device_id_type=MESH)
    pl.semaphore_signal(barrier, inc=1, device_id={"cfg": 1 - half}, device_id_type=MESH)
    pl.semaphore_wait(barrier, n)

    right, left = {"tp": (me + 1) % n}, {"tp": (me + n - 1) % n}
    hops_of = (n // 2, n // 2 - 1)

    def owner(side, k):
        return (me + n // 2 - (k - 1)) % n if side == 0 else (me - hops_of[1] + (k - 1) + n) % n

    def link(side, k, l):
        i = (side * 2 + l) * 8 + k
        src = part_ref.at[owner(side, 1), l] if k == 1 else chain.at[0, i]
        return remote(src, chain.at[1, i], s1.at[i], q1.at[i], left if side else right)

    chained = {}
    for l in range(2):
        for side in range(2):
            chained[side, 1, l] = link(side, 1, l)
            chained[side, 1, l].start()
    rows = GRID

    def mods(m):
        return [mod_ref[l, m : m + 1, :] for l in range(2)]

    def both(rows_of):
        return jnp.concatenate([rows_of(0), rows_of(1)], axis=0)

    def modulated(stream, o):
        shift, scale = mods(o), mods(o + 1)
        normed = layer_norm(stream)
        return both(
            lambda l: (normed[l * rows : (l + 1) * rows] * (1.0 + scale[l]) + shift[l]).astype(BF16)
        )

    def gated(stream, o, value):
        gate = mods(o)
        return both(
            lambda l: stream[l * rows : (l + 1) * rows] + gate[l] * value[l * rows : (l + 1) * rows]
        )

    row = row_ref[pl.ds((lax.axis_index("rs") % 4) * 8 + me, 1), :]
    place = (col_ref[...] + pb_ref[...]) + row
    stream_ref[...] = jnp.dot(
        lat_ref[...].astype(BF16), pw_ref[...], preferred_element_type=F32
    ) + jnp.concatenate([place, place], axis=0)
    for k in range(2, n // 2 + 1):
        for l in range(2):
            for side in range(2):
                if k <= hops_of[side]:
                    i = (side * 2 + l) * 8 + k
                    chained[side, k - 1, l].wait_recv()
                    chain[0, i] = (
                        chain[1, i - 1].astype(F32) + part_ref[owner(side, k), l].astype(F32)
                    ).astype(BF16)
                    chained[side, k, l] = link(side, k, l)
                    chained[side, k, l].start()
    sums = []
    for l in range(2):
        total = part_ref[me, l].astype(F32)
        for side in (1, 0):
            k = hops_of[side]
            chained[side, k, l].wait_recv()
            total = total + chain[1, (side * 2 + l) * 8 + k].astype(F32)
        sums.append(total)
    total = jnp.concatenate(sums, axis=0)
    stream = gated(stream_ref[...], 2, total + ob_ref[...])
    stream_ref[...] = stream
    gathered[me] = modulated(stream, 3)

    def hop(k):
        held_r, held_l = (me - (k - 1) + n) % n, (me + (k - 1)) % n
        out = [remote(gathered.at[held_r], gathered.at[held_r], sr.at[k], qr.at[k], right)]
        if k < n // 2:
            out.append(remote(gathered.at[held_l], gathered.at[held_l], sl.at[k], ql.at[k], left))
        for c in out:
            c.start()
        return out

    def units(x):
        pre = jnp.dot(x, up_ref[...], preferred_element_type=F32) + upb_ref[...]
        hid = jax.nn.gelu(pre, approximate=True).astype(BF16)
        return jnp.dot(hid, down_ref[...], preferred_element_type=F32).astype(BF16)

    flying = []

    def give(k, value):
        held[k] = value
        peer = (me - k + n) % n
        c = remote(held.at[k], r2.at[k], s2.at[k], q2.at[k], {"tp": peer})
        c.start()
        flying.append((k, c))

    hops = hop(1)
    own[...] = units(gathered[me])
    for k in range(1, n // 2 + 1):
        for c in hops:
            c.wait()
        if k < n // 2:
            hops = hop(k + 1)
            x = jnp.concatenate([gathered[(me - k + n) % n], gathered[(me + k) % n]], axis=0)
            y = units(x)
            give(k, y[: 2 * rows])
            give(n - k, y[2 * rows :])
        else:
            give(k, units(gathered[(me - k + n) % n]))

    for c in chained.values():
        c.wait_send()
    total = own[...].astype(F32)
    for k, c in flying:
        c.wait()
        total = total + r2[k].astype(F32)
    stream = gated(stream_ref[...], 5, total + downb_ref[...])
    value = jnp.dot(modulated(stream, 6), fw_ref[...], preferred_element_type=F32) + fb_ref[...]
    noise[...] = value
    c = remote(noise, other, s3, q3, {"cfg": 1 - half})
    c.start()
    c.wait()
    theirs = other[...]
    first = half == 0
    conditional = jnp.where(first, value, theirs)
    unconditional = jnp.where(first, theirs, value)
    guided = unconditional + GUIDANCE * (conditional - unconditional)
    out_ref[...] = c0_ref[...] * lat_ref[...] + c1_ref[...] * guided


def feed(n, *operands):
    vmem = pl.BlockSpec(memory_space=pltpu.VMEM)
    dma = pltpu.SemaphoreType.DMA
    rows = 2 * GRID
    return pl.pallas_call(
        functools.partial(feed_kernel, n),
        out_shape=jax.ShapeDtypeStruct((rows, 16), F32),
        in_specs=[vmem] * len(operands),
        out_specs=vmem,
        scratch_shapes=[
            pltpu.VMEM((2, 32, GRID, D), BF16),
            pltpu.VMEM((n, rows, D), BF16),
            pltpu.VMEM((n, rows, D), BF16),
            pltpu.VMEM((n, rows, D), BF16),
            pltpu.VMEM((rows, D), F32),
            pltpu.VMEM((rows, D), BF16),
            pltpu.VMEM((rows, 16), F32),
            pltpu.VMEM((rows, 16), F32),
        ] + [dma((32,))] * 2 + [dma((n,))] * 6 + [dma(()), dma(())],
        compiler_params=pltpu.CompilerParams(
            collective_id=1, has_side_effects=True, vmem_limit_bytes=60000000
        ),
        name="feed",
    )(*operands)


def per_device(
    latents, timesteps, labels, solver_table, time_table, label_table, patch_weight, patch_bias,
    modulation_weight, modulation_bias, heads_weight, heads_bias, output_weight, output_bias,
    up_weight, up_bias, down_weight, down_bias, final_weight, final_bias,
):
    tp_n, rs_n = lax.axis_size("tp"), lax.axis_size("rs")
    tp, half, rs = lax.axis_index("tp"), lax.axis_index("cfg"), lax.axis_index("rs")
    group, quarter = rs // 4, rs % 4
    classes = label_table.shape[0] - 1
    local, latents_dev, patch = latents.shape
    share = local // tp_n

    class_ids = jnp.where(half == 0, labels.reshape(-1), classes)
    step_onehot = jax.nn.one_hot(timesteps.reshape(-1), time_table.shape[0], dtype=BF16)
    class_onehot = jax.nn.one_hot(class_ids, classes + 1, dtype=BF16)
    cond = jnp.dot(step_onehot, time_table, preferred_element_type=F32) + jnp.dot(
        class_onehot, label_table, preferred_element_type=F32
    )
    mine = D // tp_n
    cond = jnp.pad(cond, ((0, 0), (0, 2 * LANES - mine)))
    mrows = modulation_weight.shape[0]
    mw = jnp.transpose(modulation_weight.reshape(mrows, tp_n, mine), (1, 0, 2))
    mw = jnp.pad(mw, ((0, 0), (0, LANES - mrows), (0, 2 * LANES - mine)))
    mb = jnp.pad(modulation_bias, (0, LANES - mrows)).reshape(1, LANES)
    lat_t = jnp.transpose(latents.astype(BF16), (1, 2, 0))
    mod, lat_all = conditioning(cond, mw, mb, lat_t, tp_n, rs_n)

    row_np, col_np = position_tables()
    row, col = jnp.asarray(row_np), jnp.asarray(col_np)
    patch_bias = patch_bias.reshape(1, D)
    fill = 2 * LANES - mine
    w = jnp.pad(heads_weight[0], ((0, 0), (0, 0), (0, fill))).reshape(D, 6 * LANES)
    b = jnp.pad(heads_bias[0], ((0, 0), (0, fill))).reshape(1, 6 * LANES)
    partial = attention(lat_all, patch_weight, patch_bias, col, row, mod, w, b, output_weight[0])

    own = lax.dynamic_slice_in_dim(latents, tp * share, share, 0)
    own = jnp.transpose(own, (1, 0, 2)).reshape(2 * share, patch)
    step_own = lax.dynamic_index_in_dim(timesteps, group, 0, keepdims=False)
    hot = jax.nn.one_hot(step_own, solver_table.shape[0], dtype=F32)
    coef = jnp.dot(hot, solver_table, precision=lax.Precision.HIGHEST)
    coef = jnp.repeat(coef, share, axis=0)
    out = feed(
        tp_n, partial, own, patch_weight, patch_bias, col, row, mod, output_bias, up_weight[0],
        up_bias, down_weight[0], down_bias, final_weight, final_bias.reshape(1, patch),
        coef[:, 0:1], coef[:, 1:2],
    )
    kept = lax.dynamic_slice_in_dim(out, half * (patch // 2), patch // 2, 1)
    return jnp.transpose(kept.reshape(latents_dev, share, patch // 2), (1, 0, 2))


def solution(mesh):
    in_specs = (
        P("rs", None, None), P(), P(), P(), P(None, "tp"), P(None, "tp"), P(), P(),
        P(("rs", "tp"), None), P(("rs", "tp")), P(None, None, None, "tp"), P(None, None, "tp"),
        P(None, "tp", None), P(), P(None, None, "tp"), P(None, "tp"), P(None, "tp", None), P(),
        P(), P(),
    )
    return jax.shard_map(
        per_device, mesh=mesh, in_specs=in_specs,
        out_specs=P(("rs", "tp"), None, "cfg"), check_vma=False,
    )
```

```python
import functools

import jax
import jax.numpy as jnp
import numpy as np
from jax import lax
from jax.experimental import pallas as pl
from jax.experimental.pallas import tpu as pltpu
from jax.sharding import PartitionSpec as P

HEAD_DIM = 72
GRID = 32
D = 1152
LANES = 128
GUIDANCE = 4.0
MESH = pl.DeviceIdType.MESH
F32, BF16 = jnp.float32, jnp.bfloat16


def remote(src, dst, send, recv, device):
    return pltpu.make_async_remote_copy(
        src_ref=src, dst_ref=dst, send_sem=send, recv_sem=recv, device_id=device, device_id_type=MESH
    )


def layer_norm(values):
    centre = values - jnp.mean(values, axis=-1, keepdims=True)
    spread = jnp.mean(centre * centre, axis=-1, keepdims=True)
    return centre * lax.rsqrt(spread + 1e-06)


def position_tables():
    count = D // 4
    frequency = 1.0 / 10000.0 ** (np.arange(count, dtype=np.float64) / count)
    angle = np.arange(GRID, dtype=np.float64)[:, None] * frequency[None, :]
    half = np.concatenate([np.sin(angle), np.cos(angle)], axis=1)
    zero = np.zeros_like(half)
    row = np.concatenate([half, zero], axis=1).astype(np.float32)
    col = np.concatenate([zero, half], axis=1).astype(np.float32)
    return row, col


def conditioning_kernel(
    tp_n, rs_n, cond_ref, w_ref, b_ref, lat_ref, out_ref, latall_ref,
    cbuf, part, pbuf, blk, gbuf, obuf, lbuf, s1, r1, s2, r2, s3, r3, s4, r4, s5, r5,
):
    tp, rs = lax.axis_index("tp"), lax.axis_index("rs")
    quarter, group, groups = rs % 4, rs // 4, rs_n // 4
    barrier = pltpu.get_barrier_semaphore()

    def at_tp(d):
        return {"tp": (tp + d) % tp_n}

    def at_quarter(d):
        return {"rs": group * 4 + (quarter + d) % 4}

    def at_group(d):
        return {"rs": ((group + d) % groups) * 4 + quarter}

    for d in range(1, tp_n):
        pl.semaphore_signal(barrier, inc=1, device_id=at_tp(d), device_id_type=MESH)
    for d in range(1, groups):
        pl.semaphore_signal(barrier, inc=1, device_id=at_group(d), device_id_type=MESH)
    for d in range(1, 4):
        pl.semaphore_signal(barrier, inc=1, device_id=at_quarter(d), device_id_type=MESH)
    pl.semaphore_wait(barrier, tp_n - 1 + groups - 1 + 3)

    first = []
    for d in range(1, tp_n):
        c = remote(cond_ref, cbuf.at[tp], s1.at[d], r1.at[d], at_tp(d))
        c.start()
        first.append(c)
    lats = []
    for d in range(1, 4):
        c = remote(lat_ref, lbuf.at[d], s4.at[d], r4.at[d], at_quarter(d))
        c.start()
        lats.append(c)
    cbuf[tp] = cond_ref[...]
    latall_ref[0] = lat_ref[...]
    for c in first:
        c.wait()
    v = jnp.concatenate([cbuf[t] for t in range(tp_n)], axis=1)
    act = (v / (1.0 + jnp.exp(-v))).astype(BF16)
    total = lax.dot_general(
        act, w_ref[...], (((1,), (1,)), ((), ())), preferred_element_type=F32
    ) + b_ref[...]
    part[...] = total
    second = []
    for d in range(1, tp_n):
        c = remote(part, pbuf.at[tp], s2.at[d], r2.at[d], at_tp(d))
        c.start()
        second.append(c)
    pbuf[tp] = total
    for d in range(1, 4):
        lats[d - 1].wait()
        latall_ref[d] = lbuf[d]
    for c in second:
        c.wait()
    rows = jnp.concatenate([pbuf[t] for t in range(tp_n)], axis=1)
    width = rows.shape[1]
    rows = jnp.concatenate([rows, jnp.zeros((rows.shape[0], 3 * LANES - width), F32)], axis=1)
    for g in range(groups):
        blk[g] = rows[2 * g : 2 * g + 2, :]
    third = []
    for d in range(1, groups):
        c = remote(blk.at[(group + d) % groups], gbuf.at[group], s3.at[d], r3.at[d], at_group(d))
        c.start()
        third.append(c)
    gbuf[group] = blk[group]
    for c in third:
        c.wait()
    fourth = []
    for d in range(1, 4):
        c = remote(gbuf, obuf.at[quarter], s5.at[d], r5.at[d], at_quarter(d))
        c.start()
        fourth.append(c)
    obuf[quarter] = gbuf[...]
    for c in fourth:
        c.wait()
    for l in range(2):
        out_ref[l] = jnp.concatenate([obuf[q, :, l, :][:, :width] for q in range(4)], axis=1)


def conditioning(cond, weight, bias, lat, tp_n, rs_n):
    n, share = cond.shape[0], weight.shape[0]
    wide, groups = 3 * LANES, rs_n // 4
    vmem = pl.BlockSpec(memory_space=pltpu.VMEM)
    dma = pltpu.SemaphoreType.DMA
    return pl.pallas_call(
        functools.partial(conditioning_kernel, tp_n, rs_n),
        out_shape=(
            jax.ShapeDtypeStruct((2, groups, D), F32),
            jax.ShapeDtypeStruct((4,) + lat.shape, BF16),
        ),
        in_specs=[vmem] * 4,
        out_specs=(vmem, vmem),
        scratch_shapes=[
            pltpu.VMEM((tp_n,) + cond.shape, F32),
            pltpu.VMEM((n, share), F32),
            pltpu.VMEM((tp_n, n, share), F32),
            pltpu.VMEM((groups, 2, wide), F32),
            pltpu.VMEM((groups, 2, wide), F32),
            pltpu.VMEM((4, groups, 2, wide), F32),
            pltpu.VMEM((4,) + lat.shape, BF16),
            dma((tp_n,)), dma((tp_n,)), dma((tp_n,)), dma((tp_n,)),
            dma((groups,)), dma((groups,)), dma((4,)), dma((4,)), dma((4,)), dma((4,)),
        ],
        compiler_params=pltpu.CompilerParams(collective_id=0, has_side_effects=True),
        name="conditioning",
    )(cond, weight, bias, lat)


def attention_kernel(lat_ref, pw_ref, pb_ref, col_ref, row_ref, mod_ref, w_ref, b_ref,
                     wo_ref, out_ref, normed, kv):
    tile, wide = 256, 2 * HEAD_DIM
    quarter = lax.axis_index("rs") % 4

    def project(i):
        return lax.dot_general(
            normed[...], w_ref[i], (((1,), (1,)), ((), ())), preferred_element_type=F32
        ) + b_ref[i : i + 1, :]

    def fill(latent, slot):
        emb = lax.dot_general(
            lat_ref[slot, latent], pw_ref[...], (((0,), (0,)), ((), ())),
            preferred_element_type=F32,
        )
        shift, scale = mod_ref[latent, 0:1, :], 1.0 + mod_ref[latent, 1:2, :]
        col = col_ref[...] + pb_ref[...]
        place = pl.multiple_of(((quarter + 4 - slot) % 4) * 8, 8)
        row = row_ref[pl.ds(place, 8), :]
        for i in range(tile // GRID):
            stream = (emb[i * GRID : (i + 1) * GRID] + col) + row[i : i + 1, :]
            normed[i * GRID : (i + 1) * GRID, :] = (
                layer_norm(stream) * scale + shift
            ).astype(BF16)
        for i in range(2):
            kv[i, pl.ds(pl.multiple_of(slot * tile, tile), tile), :] = project(i + 1).astype(BF16)

    @pl.loop(0, 2)
    def _(latent):
        @pl.loop(0, 4)
        def _(step):
            fill(latent, 3 - step)

        queries = project(0)
        lane = lax.broadcasted_iota(jnp.int32, (tile, wide), 1)
        heads = []
        for h in range(2):
            inside = (lane >= h * HEAD_DIM) & (lane < (h + 1) * HEAD_DIM)
            q = jnp.where(inside, queries, 0.0).astype(BF16)
            scores = lax.dot_general(
                q, kv[0], (((1,), (1,)), ((), ())), preferred_element_type=F32
            ) * HEAD_DIM ** (-0.5)
            exponent = jnp.exp(scores - jnp.max(scores, axis=-1, keepdims=True))
            row_total = jnp.sum(exponent, axis=-1, keepdims=True)
            weighted = jnp.dot(exponent.astype(BF16), kv[1], preferred_element_type=F32)
            heads.append(weighted / row_total)
        attended = jnp.where(lane < HEAD_DIM, heads[0], heads[1]).astype(BF16)
        result = jnp.dot(attended, wo_ref[...], preferred_element_type=F32).astype(BF16)
        for t in range(8):
            out_ref[t, latent] = result[t * GRID : (t + 1) * GRID, :]


def attention(*operands):
    vmem = pl.BlockSpec(memory_space=pltpu.VMEM)
    return pl.pallas_call(
        attention_kernel,
        out_shape=jax.ShapeDtypeStruct((8, 2, GRID, D), BF16),
        in_specs=[vmem] * len(operands),
        out_specs=vmem,
        scratch_shapes=[pltpu.VMEM((256, D), BF16), pltpu.VMEM((2, 1024, 2 * HEAD_DIM), BF16)],
        compiler_params=pltpu.CompilerParams(vmem_limit_bytes=60000000),
        name="attention",
    )(*operands)


def feed_kernel(
    n, part_ref, lat_ref, pw_ref, pb_ref, col_ref, row_ref, mod_ref, ob_ref, up_ref, upb_ref,
    down_ref, downb_ref, fw_ref, fb_ref, c0_ref, c1_ref, out_ref,
    chain, flight, gathered, held, stream_ref, noise, other,
    s1, q1, sg, qg, s2, q2, s3, q3,
):
    me, half = lax.axis_index("tp"), lax.axis_index("cfg")
    barrier = pltpu.get_barrier_semaphore()
    for d in range(1, n):
        pl.semaphore_signal(barrier, inc=1, device_id={"tp": (me + d) % n}, device_id_type=MESH)
    pl.semaphore_signal(barrier, inc=1, device_id={"cfg": 1 - half}, device_id_type=MESH)
    pl.semaphore_wait(barrier, n)

    right, left = {"tp": (me + 1) % n}, {"tp": (me + n - 1) % n}
    far = n // 2

    def hops_of(side, l):
        return far if side == l else far - 1

    def owner(side, l, k):
        away = hops_of(side, l) - (k - 1)
        return (me + away) % n if side == 0 else (me - away + n) % n

    def chain_start(source, flight, sems, l, side):
        i = (side * 2 + l) * 8 + 1
        c = remote(source.at[owner(side, l, 1), l], flight.at[1, i], sems[0].at[i], sems[1].at[i],
                   left if side else right)
        c.start()
        return c

    def chain_step(source, flight, sems, chained, k, l, side):
        i = (side * 2 + l) * 8 + k
        chained[side, k - 1, l].wait_recv()
        flight[0, i] = (
            flight[1, i - 1].astype(F32) + source[owner(side, l, k), l].astype(F32)
        ).astype(BF16)
        c = remote(flight.at[0, i], flight.at[1, i], sems[0].at[i], sems[1].at[i],
                   left if side else right)
        c.start()
        chained[side, k, l] = c

    def chain_end(source, flight, chained):
        sums = []
        for l in range(2):
            total = source[me, l].astype(F32)
            for side in range(2):
                k = hops_of(side, l)
                chained[side, k, l].wait_recv()
                total = total + flight[1, (side * 2 + l) * 8 + k].astype(F32)
            sums.append(total)
        return jnp.concatenate(sums, axis=0)

    one, two = (s1, q1), (s2, q2)
    chained = {}
    for l in range(2):
        for side in range(2):
            chained[side, 1, l] = chain_start(part_ref, chain, one, l, side)
    rows = GRID

    def mods(m):
        return [mod_ref[l, m : m + 1, :] for l in range(2)]

    def both(rows_of):
        return jnp.concatenate([rows_of(0), rows_of(1)], axis=0)

    def modulated(stream, o):
        shift, scale = mods(o), mods(o + 1)
        normed = layer_norm(stream)
        return both(
            lambda l: (normed[l * rows : (l + 1) * rows] * (1.0 + scale[l]) + shift[l]).astype(BF16)
        )

    def gated(stream, o, value):
        gate = mods(o)
        return both(
            lambda l: stream[l * rows : (l + 1) * rows] + gate[l] * value[l * rows : (l + 1) * rows]
        )

    row = row_ref[pl.ds((lax.axis_index("rs") % 4) * 8 + me, 1), :]
    place = (col_ref[...] + pb_ref[...]) + row
    stream_ref[...] = jnp.dot(
        lat_ref[...].astype(BF16), pw_ref[...], preferred_element_type=F32
    ) + jnp.concatenate([place, place], axis=0)
    for k in range(2, far + 1):
        for l in range(2):
            for side in range(2):
                if k <= hops_of(side, l):
                    chain_step(part_ref, chain, one, chained, k, l, side)
    total = chain_end(part_ref, chain, chained)
    stream = gated(stream_ref[...], 2, total + ob_ref[...])
    stream_ref[...] = stream
    second = modulated(stream, 3)
    gathered[me, 0], gathered[me, 1] = second[:rows], second[rows:]

    def hop(k):
        out = []
        for l in range(2):
            for side in range(2):
                if k <= hops_of(side, l):
                    b = (me - (k - 1) + n) % n if side == 0 else (me + (k - 1)) % n
                    i = (side * 2 + l) * 8 + k
                    c = remote(gathered.at[b, l], gathered.at[b, l], sg.at[i], qg.at[i],
                               left if side else right)
                    c.start()
                    out.append(c)
        return out

    def units(blocks):
        x = jnp.concatenate([gathered[b, l] for b in blocks for l in range(2)], axis=0)
        pre = lax.dot_general(
            x, up_ref[...], (((1,), (1,)), ((), ())), preferred_element_type=F32
        ) + upb_ref[...]
        hid = jax.nn.gelu(pre, approximate=True).astype(BF16)
        y = jnp.dot(hid, down_ref[...], preferred_element_type=F32).astype(BF16)
        for j, b in enumerate(blocks):
            for l in range(2):
                held[b, l] = y[(2 * j + l) * rows : (2 * j + l + 1) * rows]

    hops = hop(1)
    units([me])
    back = {}
    for k in range(1, far):
        for c in hops:
            c.wait()
        hops = hop(k + 1)
        units([(me - k + n) % n, (me + k) % n])
    for l in range(2):
        back[1 - l, 1, l] = chain_start(held, flight, two, l, 1 - l)
    for c in hops:
        c.wait()
    units([(me + far) % n])
    for l in range(2):
        back[l, 1, l] = chain_start(held, flight, two, l, l)
    for k in range(2, far + 1):
        for short in (True, False):
            for l in range(2):
                side = 1 - l if short else l
                if k <= hops_of(side, l):
                    chain_step(held, flight, two, back, k, l, side)
    total = chain_end(held, flight, back)
    for c in list(chained.values()) + list(back.values()):
        c.wait_send()
    stream = gated(stream_ref[...], 5, total + downb_ref[...])
    value = lax.dot_general(
        modulated(stream, 6), fw_ref[...], (((1,), (1,)), ((), ())), preferred_element_type=F32
    ) + fb_ref[...]
    noise[...] = value
    c = remote(noise, other, s3, q3, {"cfg": 1 - half})
    c.start()
    c.wait()
    theirs = other[...]
    first = half == 0
    conditional = jnp.where(first, value, theirs)
    unconditional = jnp.where(first, theirs, value)
    guided = unconditional + GUIDANCE * (conditional - unconditional)
    out_ref[...] = c0_ref[...] * lat_ref[...] + c1_ref[...] * guided


def feed(n, *operands):
    vmem = pl.BlockSpec(memory_space=pltpu.VMEM)
    dma = pltpu.SemaphoreType.DMA
    rows = 2 * GRID
    return pl.pallas_call(
        functools.partial(feed_kernel, n),
        out_shape=jax.ShapeDtypeStruct((rows, 16), F32),
        in_specs=[vmem] * len(operands),
        out_specs=vmem,
        scratch_shapes=[
            pltpu.VMEM((2, 32, GRID, D), BF16),
            pltpu.VMEM((2, 32, GRID, D), BF16),
            pltpu.VMEM((n, 2, GRID, D), BF16),
            pltpu.VMEM((n, 2, GRID, D), BF16),
            pltpu.VMEM((rows, D), F32),
            pltpu.VMEM((rows, 16), F32),
            pltpu.VMEM((rows, 16), F32),
        ] + [dma((32,))] * 6 + [dma(()), dma(())],
        compiler_params=pltpu.CompilerParams(
            collective_id=1, has_side_effects=True, vmem_limit_bytes=60000000
        ),
        name="feed",
    )(*operands)


def per_device(
    latents, timesteps, labels, solver_table, time_table, label_table, patch_weight, patch_bias,
    modulation_weight, modulation_bias, heads_weight, heads_bias, output_weight, output_bias,
    up_weight, up_bias, down_weight, down_bias, final_weight, final_bias,
):
    tp_n, rs_n = lax.axis_size("tp"), lax.axis_size("rs")
    tp, half, rs = lax.axis_index("tp"), lax.axis_index("cfg"), lax.axis_index("rs")
    group, quarter = rs // 4, rs % 4
    classes = label_table.shape[0] - 1
    local, latents_dev, patch = latents.shape
    share = local // tp_n

    class_ids = jnp.where(half == 0, labels.reshape(-1), classes)
    step_onehot = jax.nn.one_hot(timesteps.reshape(-1), time_table.shape[0], dtype=BF16)
    class_onehot = jax.nn.one_hot(class_ids, classes + 1, dtype=BF16)
    cond = jnp.dot(step_onehot, time_table, preferred_element_type=F32) + jnp.dot(
        class_onehot, label_table, preferred_element_type=F32
    )
    lat_t = jnp.transpose(latents.astype(BF16), (1, 2, 0))
    mod, lat_all = conditioning(
        cond, modulation_weight, modulation_bias.reshape(1, -1), lat_t, tp_n, rs_n
    )

    row_np, col_np = position_tables()
    row, col = jnp.asarray(row_np), jnp.asarray(col_np)
    patch_bias = patch_bias.reshape(1, D)
    w = jnp.transpose(heads_weight[0], (1, 2, 0))
    b = heads_bias[0]
    partial = attention(lat_all, patch_weight, patch_bias, col, row, mod, w, b, output_weight[0])

    own = lax.dynamic_slice_in_dim(latents, tp * share, share, 0)
    own = jnp.transpose(own, (1, 0, 2)).reshape(2 * share, patch)
    step_own = lax.dynamic_index_in_dim(timesteps, group, 0, keepdims=False)
    hot = jax.nn.one_hot(step_own, solver_table.shape[0], dtype=F32)
    coef = jnp.dot(hot, solver_table, precision=lax.Precision.HIGHEST)
    coef = jnp.repeat(coef, share, axis=0)
    out = feed(
        tp_n, partial, own, patch_weight, patch_bias, col, row, mod, output_bias,
        jnp.transpose(up_weight[0]), up_bias, down_weight[0], down_bias,
        jnp.transpose(final_weight), final_bias.reshape(1, patch),
        coef[:, 0:1], coef[:, 1:2],
    )
    kept = lax.dynamic_slice_in_dim(out, half * (patch // 2), patch // 2, 1)
    return jnp.transpose(kept.reshape(latents_dev, share, patch // 2), (1, 0, 2))


def solution(mesh):
    in_specs = (
        P("rs", None, None), P(), P(), P(), P(None, "tp"), P(None, "tp"), P(), P(),
        P(("rs", "tp"), None), P(("rs", "tp")), P(None, None, None, "tp"), P(None, None, "tp"),
        P(None, "tp", None), P(), P(None, None, "tp"), P(None, "tp"), P(None, "tp", None), P(),
        P(), P(),
    )
    return jax.shard_map(
        per_device, mesh=mesh, in_specs=in_specs,
        out_specs=P(("rs", "tp"), None, "cfg"), check_vma=False,
    )
```

```python
import functools

import jax
import jax.numpy as jnp
import numpy as np
from jax import lax
from jax.experimental import pallas as pl
from jax.experimental.pallas import tpu as pltpu
from jax.sharding import PartitionSpec as P

HEAD_DIM = 72
GRID = 32
D = 1152
LANES = 128
GUIDANCE = 4.0
MESH = pl.DeviceIdType.MESH
F32, BF16 = jnp.float32, jnp.bfloat16


def remote(src, dst, send, recv, device):
    return pltpu.make_async_remote_copy(
        src_ref=src, dst_ref=dst, send_sem=send, recv_sem=recv, device_id=device, device_id_type=MESH
    )


def layer_norm(values):
    centre = values - jnp.mean(values, axis=-1, keepdims=True)
    spread = jnp.mean(centre * centre, axis=-1, keepdims=True)
    return centre * lax.rsqrt(spread + 1e-06)


def position_tables():
    count = D // 4
    frequency = 1.0 / 10000.0 ** (np.arange(count, dtype=np.float64) / count)
    angle = np.arange(GRID, dtype=np.float64)[:, None] * frequency[None, :]
    half = np.concatenate([np.sin(angle), np.cos(angle)], axis=1)
    zero = np.zeros_like(half)
    row = np.concatenate([half, zero], axis=1).astype(np.float32)
    col = np.concatenate([zero, half], axis=1).astype(np.float32)
    return row, col


def conditioning_kernel(
    tp_n, rs_n, cond_ref, w_ref, b_ref, lat_ref, out_ref, latall_ref,
    cbuf, part, pbuf, blk, gbuf, obuf, lbuf, s1, r1, s2, r2, s3, r3, s4, r4, s5, r5,
):
    tp, rs = lax.axis_index("tp"), lax.axis_index("rs")
    quarter, group, groups = rs % 4, rs // 4, rs_n // 4
    barrier = pltpu.get_barrier_semaphore()

    def at_tp(d):
        return {"tp": (tp + d) % tp_n}

    def at_quarter(d):
        return {"rs": group * 4 + (quarter + d) % 4}

    def at_group(d):
        return {"rs": ((group + d) % groups) * 4 + quarter}

    for d in range(1, tp_n):
        pl.semaphore_signal(barrier, inc=1, device_id=at_tp(d), device_id_type=MESH)
    for d in range(1, groups):
        pl.semaphore_signal(barrier, inc=1, device_id=at_group(d), device_id_type=MESH)
    for d in range(1, 4):
        pl.semaphore_signal(barrier, inc=1, device_id=at_quarter(d), device_id_type=MESH)
    pl.semaphore_wait(barrier, tp_n - 1 + groups - 1 + 3)

    first = []
    for d in range(1, tp_n):
        c = remote(cond_ref, cbuf.at[tp], s1.at[d], r1.at[d], at_tp(d))
        c.start()
        first.append(c)
    lats = []
    for d in range(1, 4):
        c = remote(lat_ref, lbuf.at[d], s4.at[d], r4.at[d], at_quarter(d))
        c.start()
        lats.append(c)
    cbuf[tp] = cond_ref[...]
    latall_ref[0] = lat_ref[...]
    for c in first:
        c.wait()
    v = jnp.concatenate([cbuf[t] for t in range(tp_n)], axis=1)
    act = (v / (1.0 + jnp.exp(-v))).astype(BF16)
    total = lax.dot_general(
        act, w_ref[...], (((1,), (1,)), ((), ())), preferred_element_type=F32
    ) + b_ref[...]
    part[...] = total
    second = []
    for d in range(1, tp_n):
        c = remote(part, pbuf.at[tp], s2.at[d], r2.at[d], at_tp(d))
        c.start()
        second.append(c)
    pbuf[tp] = total
    for d in range(1, 4):
        lats[d - 1].wait()
        latall_ref[d] = lbuf[d]
    for c in second:
        c.wait()
    rows = jnp.concatenate([pbuf[t] for t in range(tp_n)], axis=1)
    width = rows.shape[1]
    rows = jnp.concatenate([rows, jnp.zeros((rows.shape[0], 3 * LANES - width), F32)], axis=1)
    for g in range(groups):
        blk[g] = rows[2 * g : 2 * g + 2, :]
    third = []
    for d in range(1, groups):
        c = remote(blk.at[(group + d) % groups], gbuf.at[group], s3.at[d], r3.at[d], at_group(d))
        c.start()
        third.append(c)
    gbuf[group] = blk[group]
    for c in third:
        c.wait()
    fourth = []
    for d in range(1, 4):
        c = remote(gbuf, obuf.at[quarter], s5.at[d], r5.at[d], at_quarter(d))
        c.start()
        fourth.append(c)
    obuf[quarter] = gbuf[...]
    for c in fourth:
        c.wait()
    for l in range(2):
        out_ref[l] = jnp.concatenate([obuf[q, :, l, :][:, :width] for q in range(4)], axis=1)


def conditioning(cond, weight, bias, lat, tp_n, rs_n):
    n, share = cond.shape[0], weight.shape[0]
    wide, groups = 3 * LANES, rs_n // 4
    vmem = pl.BlockSpec(memory_space=pltpu.VMEM)
    dma = pltpu.SemaphoreType.DMA
    return pl.pallas_call(
        functools.partial(conditioning_kernel, tp_n, rs_n),
        out_shape=(
            jax.ShapeDtypeStruct((2, groups, D), F32),
            jax.ShapeDtypeStruct((4,) + lat.shape, BF16),
        ),
        in_specs=[vmem] * 4,
        out_specs=(vmem, vmem),
        scratch_shapes=[
            pltpu.VMEM((tp_n,) + cond.shape, F32),
            pltpu.VMEM((n, share), F32),
            pltpu.VMEM((tp_n, n, share), F32),
            pltpu.VMEM((groups, 2, wide), F32),
            pltpu.VMEM((groups, 2, wide), F32),
            pltpu.VMEM((4, groups, 2, wide), F32),
            pltpu.VMEM((4,) + lat.shape, BF16),
            dma((tp_n,)), dma((tp_n,)), dma((tp_n,)), dma((tp_n,)),
            dma((groups,)), dma((groups,)), dma((4,)), dma((4,)), dma((4,)), dma((4,)),
        ],
        compiler_params=pltpu.CompilerParams(collective_id=0, has_side_effects=True),
        name="conditioning",
    )(cond, weight, bias, lat)


def attention_kernel(lat_ref, pw_ref, pb_ref, col_ref, row_ref, mod_ref, w_ref, b_ref,
                     wo_ref, out_ref, normed, kv):
    tile, wide = 256, 2 * HEAD_DIM
    quarter = lax.axis_index("rs") % 4

    def project(i):
        return lax.dot_general(
            normed[...], w_ref[i], (((1,), (1,)), ((), ())), preferred_element_type=F32
        ) + b_ref[i : i + 1, :]

    def fill(latent, slot):
        emb = lax.dot_general(
            lat_ref[slot, latent], pw_ref[...], (((0,), (0,)), ((), ())),
            preferred_element_type=F32,
        )
        shift, scale = mod_ref[latent, 0:1, :], 1.0 + mod_ref[latent, 1:2, :]
        col = col_ref[...] + pb_ref[...]
        place = pl.multiple_of(((quarter + 4 - slot) % 4) * 8, 8)
        row = row_ref[pl.ds(place, 8), :]
        for i in range(tile // GRID):
            stream = (emb[i * GRID : (i + 1) * GRID] + col) + row[i : i + 1, :]
            normed[i * GRID : (i + 1) * GRID, :] = (
                layer_norm(stream) * scale + shift
            ).astype(BF16)
        for i in range(2):
            kv[i, pl.ds(pl.multiple_of(slot * tile, tile), tile), :] = project(i + 1).astype(BF16)

    @pl.loop(0, 2)
    def _(latent):
        @pl.loop(0, 4)
        def _(step):
            fill(latent, 3 - step)

        queries = project(0)
        lane = lax.broadcasted_iota(jnp.int32, (tile, wide), 1)
        heads = []
        for h in range(2):
            inside = (lane >= h * HEAD_DIM) & (lane < (h + 1) * HEAD_DIM)
            q = jnp.where(inside, queries, 0.0).astype(BF16)
            scores = lax.dot_general(
                q, kv[0], (((1,), (1,)), ((), ())), preferred_element_type=F32
            ) * HEAD_DIM ** (-0.5)
            exponent = jnp.exp(scores - jnp.max(scores, axis=-1, keepdims=True))
            row_total = jnp.sum(exponent, axis=-1, keepdims=True)
            weighted = jnp.dot(exponent.astype(BF16), kv[1], preferred_element_type=F32)
            heads.append(weighted / row_total)
        attended = jnp.where(lane < HEAD_DIM, heads[0], heads[1]).astype(BF16)
        result = jnp.dot(attended, wo_ref[...], preferred_element_type=F32).astype(BF16)
        for t in range(8):
            out_ref[t, latent] = result[t * GRID : (t + 1) * GRID, :]


def attention(*operands):
    vmem = pl.BlockSpec(memory_space=pltpu.VMEM)
    return pl.pallas_call(
        attention_kernel,
        out_shape=jax.ShapeDtypeStruct((8, 2, GRID, D), BF16),
        in_specs=[vmem] * len(operands),
        out_specs=vmem,
        scratch_shapes=[pltpu.VMEM((256, D), BF16), pltpu.VMEM((2, 1024, 2 * HEAD_DIM), BF16)],
        compiler_params=pltpu.CompilerParams(vmem_limit_bytes=60000000),
        name="attention",
    )(*operands)


def feed_kernel(
    n, part_ref, lat_ref, pw_ref, pb_ref, col_ref, row_ref, mod_ref, ob_ref, up_ref, upb_ref,
    down_ref, downb_ref, fw_ref, fb_ref, c0_ref, c1_ref, out_ref,
    chain, flight, gathered, held, stream_ref, noise, other,
    s1, q1, sg, qg, s2, q2, s3, q3,
):
    me, half = lax.axis_index("tp"), lax.axis_index("cfg")
    barrier = pltpu.get_barrier_semaphore()
    for d in range(1, n):
        pl.semaphore_signal(barrier, inc=1, device_id={"tp": (me + d) % n}, device_id_type=MESH)
    pl.semaphore_signal(barrier, inc=1, device_id={"cfg": 1 - half}, device_id_type=MESH)
    pl.semaphore_wait(barrier, n)

    right, left = {"tp": (me + 1) % n}, {"tp": (me + n - 1) % n}
    far = n // 2

    def hops_of(side, l):
        return far if side == l else far - 1

    def owner(side, l, k):
        away = hops_of(side, l) - (k - 1)
        return (me + away) % n if side == 0 else (me - away + n) % n

    size = GRID // 2
    pieces = [(l, side, p) for p in range(2) for l in range(2) for side in range(2)]

    def slot(l, side, p, k):
        return ((side * 2 + l) * 2 + p) * 4 + (k - 1)

    def piece(ref, block, l, p):
        return ref.at[block, l, pl.ds(p * size, size)]

    def send(src, dst, sems, i, side):
        c = remote(src, dst, sems[0].at[i], sems[1].at[i], left if side else right)
        c.start()
        return c

    def chain_start(source, moving, sems, l, side, p):
        i = slot(l, side, p, 1)
        return send(piece(source, owner(side, l, 1), l, p), moving.at[1, i], sems, i, side)

    def chain_step(source, moving, sems, chained, k, l, side, p):
        i = slot(l, side, p, k)
        chained[side, k - 1, l, p].wait_recv()
        mine = source[owner(side, l, k), l, p * size : (p + 1) * size, :]
        moving[0, i] = (moving[1, i - 1].astype(F32) + mine.astype(F32)).astype(BF16)
        chained[side, k, l, p] = send(moving.at[0, i], moving.at[1, i], sems, i, side)

    def chain_end(source, moving, chained):
        sums = []
        for l in range(2):
            for p in range(2):
                total = source[me, l, p * size : (p + 1) * size, :].astype(F32)
                for side in range(2):
                    k = hops_of(side, l)
                    chained[side, k, l, p].wait_recv()
                    total = total + moving[1, slot(l, side, p, k)].astype(F32)
                sums.append(total)
        return jnp.concatenate(sums, axis=0)

    one, two = (s1, q1), (s2, q2)
    chained = {}
    for l, side, p in pieces:
        chained[side, 1, l, p] = chain_start(part_ref, chain, one, l, side, p)
    rows = GRID

    def mods(m):
        return [mod_ref[l, m : m + 1, :] for l in range(2)]

    def both(rows_of):
        return jnp.concatenate([rows_of(0), rows_of(1)], axis=0)

    def modulated(stream, o):
        shift, scale = mods(o), mods(o + 1)
        normed = layer_norm(stream)
        return both(
            lambda l: (normed[l * rows : (l + 1) * rows] * (1.0 + scale[l]) + shift[l]).astype(BF16)
        )

    def gated(stream, o, value):
        gate = mods(o)
        return both(
            lambda l: stream[l * rows : (l + 1) * rows] + gate[l] * value[l * rows : (l + 1) * rows]
        )

    row = row_ref[pl.ds((lax.axis_index("rs") % 4) * 8 + me, 1), :]
    place = (col_ref[...] + pb_ref[...]) + row
    stream_ref[...] = jnp.dot(
        lat_ref[...].astype(BF16), pw_ref[...], preferred_element_type=F32
    ) + jnp.concatenate([place, place], axis=0)
    for k in range(2, far + 1):
        for l, side, p in pieces:
            if k <= hops_of(side, l):
                chain_step(part_ref, chain, one, chained, k, l, side, p)
    total = chain_end(part_ref, chain, chained)
    stream = gated(stream_ref[...], 2, total + ob_ref[...])
    stream_ref[...] = stream
    second = modulated(stream, 3)
    gathered[me, 0], gathered[me, 1] = second[:rows], second[rows:]

    hops = {}

    def hop(k):
        for l, side, p in pieces:
            if k > 1 and k - 1 <= hops_of(side, l):
                hops[side, k - 1, l, p].wait_recv()
            if k <= hops_of(side, l):
                b = (me - (k - 1) + n) % n if side == 0 else (me + (k - 1)) % n
                part = piece(gathered, b, l, p)
                hops[side, k, l, p] = send(part, part, (sg, qg), slot(l, side, p, k), side)

    def units(blocks):
        x = jnp.concatenate([gathered[b, l] for b in blocks for l in range(2)], axis=0)
        pre = lax.dot_general(
            x, up_ref[...], (((1,), (1,)), ((), ())), preferred_element_type=F32
        ) + upb_ref[...]
        hid = jax.nn.gelu(pre, approximate=True).astype(BF16)
        y = jnp.dot(hid, down_ref[...], preferred_element_type=F32).astype(BF16)
        for j, b in enumerate(blocks):
            for l in range(2):
                held[b, l] = y[(2 * j + l) * rows : (2 * j + l + 1) * rows]

    hop(1)
    units([me])
    back = {}
    for k in range(1, far):
        hop(k + 1)
        units([(me - k + n) % n, (me + k) % n])
    for l, side, p in pieces:
        if side != l:
            back[side, 1, l, p] = chain_start(held, flight, two, l, side, p)
    hop(far + 1)
    units([(me + far) % n])
    for l, side, p in pieces:
        if side == l:
            back[side, 1, l, p] = chain_start(held, flight, two, l, side, p)
    for k in range(2, far + 1):
        for short in (True, False):
            for l, side, p in pieces:
                if (side != l) == short and k <= hops_of(side, l):
                    chain_step(held, flight, two, back, k, l, side, p)
    total = chain_end(held, flight, back)
    for c in list(chained.values()) + list(hops.values()) + list(back.values()):
        c.wait_send()
    stream = gated(stream_ref[...], 5, total + downb_ref[...])
    value = lax.dot_general(
        modulated(stream, 6), fw_ref[...], (((1,), (1,)), ((), ())), preferred_element_type=F32
    ) + fb_ref[...]
    noise[...] = value
    c = remote(noise, other, s3, q3, {"cfg": 1 - half})
    c.start()
    c.wait()
    theirs = other[...]
    first = half == 0
    conditional = jnp.where(first, value, theirs)
    unconditional = jnp.where(first, theirs, value)
    guided = unconditional + GUIDANCE * (conditional - unconditional)
    out_ref[...] = c0_ref[...] * lat_ref[...] + c1_ref[...] * guided


def feed(n, *operands):
    vmem = pl.BlockSpec(memory_space=pltpu.VMEM)
    dma = pltpu.SemaphoreType.DMA
    rows = 2 * GRID
    return pl.pallas_call(
        functools.partial(feed_kernel, n),
        out_shape=jax.ShapeDtypeStruct((rows, 16), F32),
        in_specs=[vmem] * len(operands),
        out_specs=vmem,
        scratch_shapes=[
            pltpu.VMEM((2, 32, GRID // 2, D), BF16),
            pltpu.VMEM((2, 32, GRID // 2, D), BF16),
            pltpu.VMEM((n, 2, GRID, D), BF16),
            pltpu.VMEM((n, 2, GRID, D), BF16),
            pltpu.VMEM((rows, D), F32),
            pltpu.VMEM((rows, 16), F32),
            pltpu.VMEM((rows, 16), F32),
        ] + [dma((32,))] * 6 + [dma(()), dma(())],
        compiler_params=pltpu.CompilerParams(
            collective_id=1, has_side_effects=True, vmem_limit_bytes=60000000
        ),
        name="feed",
    )(*operands)


def per_device(
    latents, timesteps, labels, solver_table, time_table, label_table, patch_weight, patch_bias,
    modulation_weight, modulation_bias, heads_weight, heads_bias, output_weight, output_bias,
    up_weight, up_bias, down_weight, down_bias, final_weight, final_bias,
):
    tp_n, rs_n = lax.axis_size("tp"), lax.axis_size("rs")
    tp, half, rs = lax.axis_index("tp"), lax.axis_index("cfg"), lax.axis_index("rs")
    group, quarter = rs // 4, rs % 4
    classes = label_table.shape[0] - 1
    local, latents_dev, patch = latents.shape
    share = local // tp_n

    class_ids = jnp.where(half == 0, labels.reshape(-1), classes)
    step_onehot = jax.nn.one_hot(timesteps.reshape(-1), time_table.shape[0], dtype=BF16)
    class_onehot = jax.nn.one_hot(class_ids, classes + 1, dtype=BF16)
    cond = jnp.dot(step_onehot, time_table, preferred_element_type=F32) + jnp.dot(
        class_onehot, label_table, preferred_element_type=F32
    )
    lat_t = jnp.transpose(latents.astype(BF16), (1, 2, 0))
    mod, lat_all = conditioning(
        cond, modulation_weight, modulation_bias.reshape(1, -1), lat_t, tp_n, rs_n
    )

    row_np, col_np = position_tables()
    row, col = jnp.asarray(row_np), jnp.asarray(col_np)
    patch_bias = patch_bias.reshape(1, D)
    w = jnp.transpose(heads_weight[0], (1, 2, 0))
    b = heads_bias[0]
    partial = attention(lat_all, patch_weight, patch_bias, col, row, mod, w, b, output_weight[0])

    own = lax.dynamic_slice_in_dim(latents, tp * share, share, 0)
    own = jnp.transpose(own, (1, 0, 2)).reshape(2 * share, patch)
    step_own = lax.dynamic_index_in_dim(timesteps, group, 0, keepdims=False)
    hot = jax.nn.one_hot(step_own, solver_table.shape[0], dtype=F32)
    coef = jnp.dot(hot, solver_table, precision=lax.Precision.HIGHEST)
    coef = jnp.repeat(coef, share, axis=0)
    out = feed(
        tp_n, partial, own, patch_weight, patch_bias, col, row, mod, output_bias,
        jnp.transpose(up_weight[0]), up_bias, down_weight[0], down_bias,
        jnp.transpose(final_weight), final_bias.reshape(1, patch),
        coef[:, 0:1], coef[:, 1:2],
    )
    kept = lax.dynamic_slice_in_dim(out, half * (patch // 2), patch // 2, 1)
    return jnp.transpose(kept.reshape(latents_dev, share, patch // 2), (1, 0, 2))


def solution(mesh):
    in_specs = (
        P("rs", None, None), P(), P(), P(), P(None, "tp"), P(None, "tp"), P(), P(),
        P(("rs", "tp"), None), P(("rs", "tp")), P(None, None, None, "tp"), P(None, None, "tp"),
        P(None, "tp", None), P(), P(None, None, "tp"), P(None, "tp"), P(None, "tp", None), P(),
        P(), P(),
    )
    return jax.shard_map(
        per_device, mesh=mesh, in_specs=in_specs,
        out_specs=P(("rs", "tp"), None, "cfg"), check_vma=False,
    )
```

```python
import functools

import jax
import jax.numpy as jnp
import numpy as np
from jax import lax
from jax.experimental import pallas as pl
from jax.experimental.pallas import tpu as pltpu
from jax.sharding import PartitionSpec as P

HEAD_DIM = 72
GRID = 32
D = 1152
LANES = 128
GUIDANCE = 4.0
MESH = pl.DeviceIdType.MESH
F32, BF16 = jnp.float32, jnp.bfloat16


def remote(src, dst, send, recv, device):
    return pltpu.make_async_remote_copy(
        src_ref=src, dst_ref=dst, send_sem=send, recv_sem=recv, device_id=device, device_id_type=MESH
    )


def layer_norm(values):
    centre = values - jnp.mean(values, axis=-1, keepdims=True)
    spread = jnp.mean(centre * centre, axis=-1, keepdims=True)
    return centre * lax.rsqrt(spread + 1e-06)


def position_tables():
    count = D // 4
    frequency = 1.0 / 10000.0 ** (np.arange(count, dtype=np.float64) / count)
    angle = np.arange(GRID, dtype=np.float64)[:, None] * frequency[None, :]
    half = np.concatenate([np.sin(angle), np.cos(angle)], axis=1)
    zero = np.zeros_like(half)
    row = np.concatenate([half, zero], axis=1).astype(np.float32)
    col = np.concatenate([zero, half], axis=1).astype(np.float32)
    return row, col


def conditioning_kernel(
    tp_n, rs_n, cond_ref, w_ref, b_ref, lat_ref, out_ref, latall_ref,
    cbuf, part, pbuf, blk, gbuf, obuf, lbuf, s1, r1, s2, r2, s3, r3, s4, r4, s5, r5,
):
    tp, rs = lax.axis_index("tp"), lax.axis_index("rs")
    quarter, group, groups = rs % 4, rs // 4, rs_n // 4
    barrier = pltpu.get_barrier_semaphore()

    def at_tp(d):
        return {"tp": (tp + d) % tp_n}

    def at_quarter(d):
        return {"rs": group * 4 + (quarter + d) % 4}

    def at_group(d):
        return {"rs": ((group + d) % groups) * 4 + quarter}

    for d in range(1, tp_n):
        pl.semaphore_signal(barrier, inc=1, device_id=at_tp(d), device_id_type=MESH)
    for d in range(1, groups):
        pl.semaphore_signal(barrier, inc=1, device_id=at_group(d), device_id_type=MESH)
    for d in range(1, 4):
        pl.semaphore_signal(barrier, inc=1, device_id=at_quarter(d), device_id_type=MESH)
    pl.semaphore_wait(barrier, tp_n - 1 + groups - 1 + 3)

    first = []
    for d in range(1, tp_n):
        c = remote(cond_ref, cbuf.at[tp], s1.at[d], r1.at[d], at_tp(d))
        c.start()
        first.append(c)
    lats = []
    for d in range(1, 4):
        c = remote(lat_ref, lbuf.at[d], s4.at[d], r4.at[d], at_quarter(d))
        c.start()
        lats.append(c)
    cbuf[tp] = cond_ref[...]
    latall_ref[0] = lat_ref[...]
    for c in first:
        c.wait()
    v = jnp.concatenate([cbuf[t] for t in range(tp_n)], axis=1)
    act = (v / (1.0 + jnp.exp(-v))).astype(BF16)
    total = lax.dot_general(
        act, w_ref[...], (((1,), (1,)), ((), ())), preferred_element_type=F32
    ) + b_ref[...]
    part[...] = total
    second = []
    for d in range(1, tp_n):
        c = remote(part, pbuf.at[tp], s2.at[d], r2.at[d], at_tp(d))
        c.start()
        second.append(c)
    pbuf[tp] = total
    for d in range(1, 4):
        lats[d - 1].wait()
        latall_ref[d] = lbuf[d]
    for c in second:
        c.wait()
    rows = jnp.concatenate([pbuf[t] for t in range(tp_n)], axis=1)
    width = rows.shape[1]
    rows = jnp.concatenate([rows, jnp.zeros((rows.shape[0], 3 * LANES - width), F32)], axis=1)
    for g in range(groups):
        blk[g] = rows[2 * g : 2 * g + 2, :]
    third = []
    for d in range(1, groups):
        c = remote(blk.at[(group + d) % groups], gbuf.at[group], s3.at[d], r3.at[d], at_group(d))
        c.start()
        third.append(c)
    gbuf[group] = blk[group]
    for c in third:
        c.wait()
    fourth = []
    for d in range(1, 4):
        c = remote(gbuf, obuf.at[quarter], s5.at[d], r5.at[d], at_quarter(d))
        c.start()
        fourth.append(c)
    obuf[quarter] = gbuf[...]
    for c in fourth:
        c.wait()
    for l in range(2):
        out_ref[l] = jnp.concatenate([obuf[q, :, l, :][:, :width] for q in range(4)], axis=1)


def conditioning(cond, weight, bias, lat, tp_n, rs_n):
    n, share = cond.shape[0], weight.shape[0]
    wide, groups = 3 * LANES, rs_n // 4
    vmem = pl.BlockSpec(memory_space=pltpu.VMEM)
    dma = pltpu.SemaphoreType.DMA
    return pl.pallas_call(
        functools.partial(conditioning_kernel, tp_n, rs_n),
        out_shape=(
            jax.ShapeDtypeStruct((2, groups, D), F32),
            jax.ShapeDtypeStruct((4,) + lat.shape, BF16),
        ),
        in_specs=[vmem] * 4,
        out_specs=(vmem, vmem),
        scratch_shapes=[
            pltpu.VMEM((tp_n,) + cond.shape, F32),
            pltpu.VMEM((n, share), F32),
            pltpu.VMEM((tp_n, n, share), F32),
            pltpu.VMEM((groups, 2, wide), F32),
            pltpu.VMEM((groups, 2, wide), F32),
            pltpu.VMEM((4, groups, 2, wide), F32),
            pltpu.VMEM((4,) + lat.shape, BF16),
            dma((tp_n,)), dma((tp_n,)), dma((tp_n,)), dma((tp_n,)),
            dma((groups,)), dma((groups,)), dma((4,)), dma((4,)), dma((4,)), dma((4,)),
        ],
        compiler_params=pltpu.CompilerParams(collective_id=0, has_side_effects=True),
        name="conditioning",
    )(cond, weight, bias, lat)


def attention_kernel(lat_ref, pw_ref, pb_ref, col_ref, row_ref, mod_ref, w_ref, b_ref,
                     wo_ref, out_ref, normed, kv):
    tile, wide = 256, 2 * HEAD_DIM
    quarter = lax.axis_index("rs") % 4

    def project(i):
        return lax.dot_general(
            normed[...], w_ref[i], (((1,), (1,)), ((), ())), preferred_element_type=F32
        ) + b_ref[i]

    def fill(latent, slot):
        emb = lax.dot_general(
            lat_ref[slot, latent], pw_ref[...], (((0,), (0,)), ((), ())),
            preferred_element_type=F32,
        )
        shift, scale = mod_ref[latent, 0:1, :], 1.0 + mod_ref[latent, 1:2, :]
        col = col_ref[...] + pb_ref[...]
        place = pl.multiple_of(((quarter + 4 - slot) % 4) * 8, 8)
        row = row_ref[pl.ds(place, 8), :]
        for i in range(tile // GRID):
            stream = (emb[i * GRID : (i + 1) * GRID] + col) + row[i : i + 1, :]
            normed[i * GRID : (i + 1) * GRID, :] = (
                layer_norm(stream) * scale + shift
            ).astype(BF16)
        for i in range(2):
            kv[i, pl.ds(pl.multiple_of(slot * tile, tile), tile), :] = project(i + 1).astype(BF16)

    @pl.loop(0, 2)
    def _(latent):
        @pl.loop(0, 4)
        def _(step):
            fill(latent, 3 - step)

        queries = project(0)
        lane = lax.broadcasted_iota(jnp.int32, (tile, wide), 1)
        heads = []
        for h in range(2):
            inside = (lane >= h * HEAD_DIM) & (lane < (h + 1) * HEAD_DIM)
            q = jnp.where(inside, queries, 0.0).astype(BF16)
            scores = lax.dot_general(
                q, kv[0], (((1,), (1,)), ((), ())), preferred_element_type=F32
            ) * HEAD_DIM ** (-0.5)
            exponent = jnp.exp(scores - jnp.max(scores, axis=-1, keepdims=True))
            row_total = jnp.sum(exponent, axis=-1, keepdims=True)
            weighted = jnp.dot(exponent.astype(BF16), kv[1], preferred_element_type=F32)
            heads.append(weighted / row_total)
        attended = jnp.where(lane < HEAD_DIM, heads[0], heads[1]).astype(BF16)
        result = jnp.dot(attended, wo_ref[...], preferred_element_type=F32).astype(BF16)
        for t in range(8):
            out_ref[t, latent] = result[t * GRID : (t + 1) * GRID, :]


def attention(*operands):
    vmem = pl.BlockSpec(memory_space=pltpu.VMEM)
    return pl.pallas_call(
        attention_kernel,
        out_shape=jax.ShapeDtypeStruct((8, 2, GRID, D), BF16),
        in_specs=[vmem] * len(operands),
        out_specs=vmem,
        scratch_shapes=[pltpu.VMEM((256, D), BF16), pltpu.VMEM((2, 1024, 2 * HEAD_DIM), BF16)],
        compiler_params=pltpu.CompilerParams(vmem_limit_bytes=60000000),
        name="attention",
    )(*operands)


def feed_kernel(
    n, part_ref, lat_ref, pw_ref, pb_ref, col_ref, row_ref, mod_ref, ob_ref, up_ref, upb_ref,
    down_ref, downb_ref, fw_ref, fb_ref, c0_ref, c1_ref, out_ref,
    chain, flight, gathered, held, stream_ref, noise, other,
    s1, q1, sg, qg, s2, q2, s3, q3,
):
    me, half = lax.axis_index("tp"), lax.axis_index("cfg")
    barrier = pltpu.get_barrier_semaphore()
    for d in range(1, n):
        pl.semaphore_signal(barrier, inc=1, device_id={"tp": (me + d) % n}, device_id_type=MESH)
    pl.semaphore_signal(barrier, inc=1, device_id={"cfg": 1 - half}, device_id_type=MESH)
    pl.semaphore_wait(barrier, n)

    right, left = {"tp": (me + 1) % n}, {"tp": (me + n - 1) % n}
    far = n // 2

    def hops_of(side, l):
        return far if side == l else far - 1

    def owner(side, l, k):
        away = hops_of(side, l) - (k - 1)
        return (me + away) % n if side == 0 else (me - away + n) % n

    size = GRID // 2
    pieces = [(l, side, p) for p in range(2) for l in range(2) for side in range(2)]

    def slot(l, side, p, k):
        return ((side * 2 + l) * 2 + p) * 4 + (k - 1)

    def piece(ref, block, l, p):
        return ref.at[block, l, pl.ds(p * size, size)]

    def send(src, dst, sems, i, side):
        c = remote(src, dst, sems[0].at[i], sems[1].at[i], left if side else right)
        c.start()
        return c

    def chain_start(source, moving, sems, l, side, p):
        i = slot(l, side, p, 1)
        return send(piece(source, owner(side, l, 1), l, p), moving.at[1, i], sems, i, side)

    def chain_step(source, moving, sems, chained, k, l, side, p):
        i = slot(l, side, p, k)
        chained[side, k - 1, l, p].wait_recv()
        mine = source[owner(side, l, k), l, p * size : (p + 1) * size, :]
        moving[0, i] = (moving[1, i - 1].astype(F32) + mine.astype(F32)).astype(BF16)
        chained[side, k, l, p] = send(moving.at[0, i], moving.at[1, i], sems, i, side)

    def chain_end(source, moving, chained):
        sums = []
        for l in range(2):
            for p in range(2):
                total = source[me, l, p * size : (p + 1) * size, :].astype(F32)
                for side in range(2):
                    k = hops_of(side, l)
                    chained[side, k, l, p].wait_recv()
                    total = total + moving[1, slot(l, side, p, k)].astype(F32)
                sums.append(total)
        return jnp.concatenate(sums, axis=0)

    one, two = (s1, q1), (s2, q2)
    chained = {}
    for l, side, p in pieces:
        chained[side, 1, l, p] = chain_start(part_ref, chain, one, l, side, p)
    rows = GRID

    def mods(m):
        return [mod_ref[l, m : m + 1, :] for l in range(2)]

    def both(rows_of):
        return jnp.concatenate([rows_of(0), rows_of(1)], axis=0)

    def modulated(stream, o):
        shift, scale = mods(o), mods(o + 1)
        normed = layer_norm(stream)
        return both(
            lambda l: (normed[l * rows : (l + 1) * rows] * (1.0 + scale[l]) + shift[l]).astype(BF16)
        )

    def gated(stream, o, value):
        gate = mods(o)
        return both(
            lambda l: stream[l * rows : (l + 1) * rows] + gate[l] * value[l * rows : (l + 1) * rows]
        )

    row = row_ref[pl.ds((lax.axis_index("rs") % 4) * 8 + me, 1), :]
    place = (col_ref[...] + pb_ref[...]) + row
    stream_ref[...] = jnp.dot(
        lat_ref[...].astype(BF16), pw_ref[...], preferred_element_type=F32
    ) + jnp.concatenate([place, place], axis=0)
    for k in range(2, far + 1):
        for l, side, p in pieces:
            if k <= hops_of(side, l):
                chain_step(part_ref, chain, one, chained, k, l, side, p)
    total = chain_end(part_ref, chain, chained)
    stream = gated(stream_ref[...], 2, total + ob_ref[...])
    stream_ref[...] = stream
    second = modulated(stream, 3)
    gathered[me, 0], gathered[me, 1] = second[:rows], second[rows:]

    hops = {}

    def hop(k):
        for l, side, p in pieces:
            if k > 1 and k - 1 <= hops_of(side, l):
                hops[side, k - 1, l, p].wait_recv()
            if k <= hops_of(side, l):
                b = (me - (k - 1) + n) % n if side == 0 else (me + (k - 1)) % n
                part = piece(gathered, b, l, p)
                hops[side, k, l, p] = send(part, part, (sg, qg), slot(l, side, p, k), side)

    def units(blocks):
        x = jnp.concatenate([gathered[b, l] for b in blocks for l in range(2)], axis=0)
        pre = lax.dot_general(
            x, up_ref[...], (((1,), (1,)), ((), ())), preferred_element_type=F32
        ) + upb_ref[...]
        hid = jax.nn.gelu(pre, approximate=True).astype(BF16)
        y = jnp.dot(hid, down_ref[...], preferred_element_type=F32).astype(BF16)
        for j, b in enumerate(blocks):
            for l in range(2):
                held[b, l] = y[(2 * j + l) * rows : (2 * j + l + 1) * rows]

    hop(1)
    units([me])
    back = {}
    for k in range(1, far):
        hop(k + 1)
        units([(me - k + n) % n, (me + k) % n])
    for l, side, p in pieces:
        if side != l:
            back[side, 1, l, p] = chain_start(held, flight, two, l, side, p)
    hop(far + 1)
    units([(me + far) % n])
    for l, side, p in pieces:
        if side == l:
            back[side, 1, l, p] = chain_start(held, flight, two, l, side, p)
    for k in range(2, far + 1):
        for short in (True, False):
            for l, side, p in pieces:
                if (side != l) == short and k <= hops_of(side, l):
                    chain_step(held, flight, two, back, k, l, side, p)
    total = chain_end(held, flight, back)
    for c in list(chained.values()) + list(hops.values()) + list(back.values()):
        c.wait_send()
    stream = gated(stream_ref[...], 5, total + downb_ref[...])
    value = lax.dot_general(
        modulated(stream, 6), fw_ref[...], (((1,), (1,)), ((), ())), preferred_element_type=F32
    ) + fb_ref[...]
    noise[...] = value
    c = remote(noise, other, s3, q3, {"cfg": 1 - half})
    c.start()
    c.wait()
    theirs = other[...]
    first = half == 0
    conditional = jnp.where(first, value, theirs)
    unconditional = jnp.where(first, theirs, value)
    guided = unconditional + GUIDANCE * (conditional - unconditional)
    result = c0_ref[...] * lat_ref[...] + c1_ref[...] * guided
    width = result.shape[1] // 2
    out_ref[...] = jnp.where(first, result[:, :width], result[:, width:])


def feed(n, *operands):
    vmem = pl.BlockSpec(memory_space=pltpu.VMEM)
    dma = pltpu.SemaphoreType.DMA
    rows = 2 * GRID
    return pl.pallas_call(
        functools.partial(feed_kernel, n),
        out_shape=jax.ShapeDtypeStruct((rows, 8), F32),
        in_specs=[vmem] * len(operands),
        out_specs=vmem,
        scratch_shapes=[
            pltpu.VMEM((2, 32, GRID // 2, D), BF16),
            pltpu.VMEM((2, 32, GRID // 2, D), BF16),
            pltpu.VMEM((n, 2, GRID, D), BF16),
            pltpu.VMEM((n, 2, GRID, D), BF16),
            pltpu.VMEM((rows, D), F32),
            pltpu.VMEM((rows, 16), F32),
            pltpu.VMEM((rows, 16), F32),
        ] + [dma((32,))] * 6 + [dma(()), dma(())],
        compiler_params=pltpu.CompilerParams(
            collective_id=1, has_side_effects=True, vmem_limit_bytes=60000000
        ),
        name="feed",
    )(*operands)


def per_device(
    latents, timesteps, labels, solver_table, time_table, label_table, patch_weight, patch_bias,
    modulation_weight, modulation_bias, heads_weight, heads_bias, output_weight, output_bias,
    up_weight, up_bias, down_weight, down_bias, final_weight, final_bias,
):
    tp_n, rs_n = lax.axis_size("tp"), lax.axis_size("rs")
    tp, half, rs = lax.axis_index("tp"), lax.axis_index("cfg"), lax.axis_index("rs")
    group, quarter = rs // 4, rs % 4
    classes = label_table.shape[0] - 1
    local, latents_dev, patch = latents.shape
    share = local // tp_n

    class_ids = jnp.where(half == 0, labels.reshape(-1), classes)
    step_onehot = jax.nn.one_hot(timesteps.reshape(-1), time_table.shape[0], dtype=BF16)
    class_onehot = jax.nn.one_hot(class_ids, classes + 1, dtype=BF16)
    cond = jnp.dot(step_onehot, time_table, preferred_element_type=F32) + jnp.dot(
        class_onehot, label_table, preferred_element_type=F32
    )
    lat_t = jnp.transpose(latents.astype(BF16), (1, 2, 0))
    mod, lat_all = conditioning(
        cond, modulation_weight, modulation_bias.reshape(1, -1), lat_t, tp_n, rs_n
    )

    row_np, col_np = position_tables()
    row, col = jnp.asarray(row_np), jnp.asarray(col_np)
    patch_bias = patch_bias.reshape(1, D)
    w = jnp.transpose(heads_weight[0], (1, 2, 0))
    b = jnp.transpose(heads_bias, (1, 0, 2))
    partial = attention(lat_all, patch_weight, patch_bias, col, row, mod, w, b, output_weight[0])

    own = lax.dynamic_slice_in_dim(latents, tp * share, share, 0)
    own = jnp.transpose(own, (1, 0, 2)).reshape(2 * share, patch)
    step_own = lax.dynamic_index_in_dim(timesteps, group, 0, keepdims=False)
    hot = jax.nn.one_hot(step_own, solver_table.shape[0], dtype=F32)
    coef = jnp.dot(hot, solver_table, precision=lax.Precision.HIGHEST)
    coef = jnp.repeat(coef, share, axis=0)
    out = feed(
        tp_n, partial, own, patch_weight, patch_bias, col, row, mod, output_bias,
        jnp.transpose(up_weight[0]), up_bias, down_weight[0], down_bias,
        jnp.transpose(final_weight), final_bias.reshape(1, patch),
        coef[:, 0:1], coef[:, 1:2],
    )
    return jnp.transpose(out.reshape(latents_dev, share, patch // 2), (1, 0, 2))


def solution(mesh):
    in_specs = (
        P("rs", None, None), P(), P(), P(), P(None, "tp"), P(None, "tp"), P(), P(),
        P(("rs", "tp"), None), P(("rs", "tp")), P(None, None, None, "tp"), P(None, None, "tp"),
        P(None, "tp", None), P(), P(None, None, "tp"), P(None, "tp"), P(None, "tp", None), P(),
        P(), P(),
    )
    return jax.shard_map(
        per_device, mesh=mesh, in_specs=in_specs,
        out_specs=P(("rs", "tp"), None, "cfg"), check_vma=False,
    )
```
